32 devices in a mesh: seq: 16 (over z, y, x), fsdp: 2 (over core).
Axes of the slice: x: 2, y: 2, z: 4, core: 2. Of those that a mesh axis runs over, the one named last changes fastest.
Arguments:
- query: bfloat16 [3072, 4096], P('seq', 'fsdp'), may hold values from -6 to 6
- key: bfloat16 [3072, 4096], P('seq', 'fsdp'), may hold values from -6 to 6
- value: bfloat16 [3072, 4096], P('seq', 'fsdp'), may hold values from -6 to 6
- grad_out: bfloat16 [3072, 4096], P('seq', 'fsdp'), may hold values from -6 to 6
- short_filter: float32 [3, 7, 4096], P(None, None, 'fsdp'), may hold values from -2 to 2
- medium_filter: float32 [256, 128], P('fsdp'), may hold values from -0.5 to 0.5
Outputs:
- grad_query: bfloat16 [3072, 4096], P('seq', 'fsdp')
- grad_key: bfloat16 [3072, 4096], P('seq', 'fsdp')
- grad_value: bfloat16 [3072, 4096], P('seq', 'fsdp')
- grad_short: float32 [3, 7, 4096], P(None, None, 'fsdp')
- grad_medium: float32 [256, 128], P('fsdp')
The draws below stay inside these ranges and needn't reach their ends.
All inputs are finite; a program needn't handle non-finite values.
Results may differ from the reference program's by a relative error of at most 0.0075.
Values may be sent and summed in bfloat16 or wider, within the bound.
No kernel may reach another device: no remote copies, remote signals or barrier semaphores. Data moves between devices by JAX's collectives and lax.ppermute only.
A program may use at most 64 MiB of HBM per device.

```python
import jax
import jax.numpy as jnp
from jax import lax

D = 4096
G = 256
SHORT = 7
LONG = 128
LEN = 3072


def levels(stream_key, extent, cuts, least, top_value):
    factor_of, own = 1.0, jax.random.fold_in(stream_key, 6)
    for axis_at, blocks in cuts:
        heights = jnp.exp(jax.random.uniform(jax.random.fold_in(own, axis_at), (blocks,), jnp.float32, least / len(cuts), top_value / len(cuts)))
        factor_of = factor_of * jnp.repeat(heights, extent[axis_at] // blocks).reshape([-1 if axis == axis_at else 1 for axis in range(len(extent))])
    return factor_of


def centred(rng, shape, width, reach, cuts=(), dtype=jnp.bfloat16):
    drawn = width * jax.random.normal(rng, shape, jnp.float32)
    if cuts:
        drawn = drawn * levels(rng, shape, cuts, -0.22, 0.18)
    return jnp.clip(drawn, -reach, reach).astype(dtype)


def setup_inputs(seed: int = 0) -> dict:
    key_list = jax.random.split(jax.random.key(seed), 7)
    return {
        "query": centred(key_list[0], (LEN, D), 1.0, 6.0, ((0, 16), (1, 2))),
        "key": centred(key_list[1], (LEN, D), 1.0, 6.0, ((0, 16), (1, 2))),
        "value": centred(key_list[2], (LEN, D), 1.0, 6.0, ((0, 16), (1, 2))),
        "grad_out": centred(key_list[3], (LEN, D), 1.0, 6.0, ((0, 16), (1, 2))),
        "short_filter": centred(key_list[4], (3, SHORT, D), SHORT ** -0.5, 2.0, ((2, 2),), jnp.float32),
        "medium_filter": centred(key_list[5], (G, LONG), LONG ** -0.5, 0.5, ((0, 2),), jnp.float32),
    }


def delayed(field, amount):
    return jnp.pad(field, ((amount, 0), (0, 0)))[:field.shape[0]]


def advanced(field, amount):
    return jnp.pad(field, ((0, amount), (0, 0)))[amount:]


def short_causal(field, weights):
    total = jnp.zeros(field.shape, jnp.float32)
    for index in range(SHORT):
        total = total + weights[index] * delayed(field, index)
    return total


def short_anticausal(field, weights):
    total = jnp.zeros(field.shape, jnp.float32)
    for index in range(SHORT):
        total = total + weights[index] * advanced(field, index)
    return total


def short_gradient(gradient, field):
    return jnp.stack([jnp.sum(gradient * delayed(field, index), axis=0) for index in range(SHORT)])


def rounded(field):
    return lax.optimization_barrier(field.astype(jnp.bfloat16)).astype(jnp.float32)


def reference(query, key, value, grad_out, short_filter, medium_filter):
    nfft = 1 << (LEN + LONG - 1).bit_length()
    blocks = D // G

    def split(field):
        return jnp.transpose(field.reshape(LEN, blocks, G), (1, 0, 2))

    def spectrum(field):
        return jnp.fft.rfft(field, n=nfft, axis=0)

    def inverse(field):
        return jnp.fft.irfft(field, n=nfft, axis=0)

    short_taps = jnp.transpose(short_filter.reshape(3, SHORT, blocks, G), (2, 0, 1, 3))
    long_taps = rounded(medium_filter).T
    long_spectrum = spectrum(long_taps)

    def one_block(operands):
        query_blk, key_blk, value_blk, grad_blk, taps_blk = operands
        query_f = query_blk.astype(jnp.float32)
        key_f = key_blk.astype(jnp.float32)
        value_f = value_blk.astype(jnp.float32)
        grad_f = grad_blk.astype(jnp.float32)
        query_short = short_causal(query_f, taps_blk[0])
        key_short = short_causal(key_f, taps_blk[1])
        value_short = short_causal(value_f, taps_blk[2])
        gated = rounded(key_short * value_short)
        gated_spec = spectrum(gated)
        signal = inverse(gated_spec * long_spectrum)[:LEN]
        grad_gated_in = rounded(grad_f * query_short)
        grad_qshort = rounded(grad_f * signal)
        grad_spec = spectrum(grad_gated_in)
        grad_gated = inverse(grad_spec * jnp.conj(long_spectrum))[:LEN]
        grad_kshort = rounded(grad_gated * value_short)
        grad_vshort = rounded(grad_gated * key_short)
        grad_q = short_anticausal(grad_qshort, taps_blk[0]).astype(jnp.bfloat16)
        grad_k = short_anticausal(grad_kshort, taps_blk[1]).astype(jnp.bfloat16)
        grad_v = short_anticausal(grad_vshort, taps_blk[2]).astype(jnp.bfloat16)
        short_part = jnp.stack([short_gradient(grad_qshort, query_f), short_gradient(grad_kshort, key_f), short_gradient(grad_vshort, value_f)])
        medium_part = inverse(grad_spec * jnp.conj(gated_spec))[:LONG]
        return grad_q, grad_k, grad_v, short_part, medium_part

    grad_q, grad_k, grad_v, short_parts, medium_parts = lax.map(one_block, (split(query), split(key), split(value), split(grad_out), short_taps))

    def joined(field):
        return jnp.transpose(field, (1, 0, 2)).reshape(LEN, D)

    grad_short = jnp.transpose(short_parts, (1, 2, 0, 3)).reshape(3, SHORT, D)
    grad_medium = jnp.sum(medium_parts, axis=0).T
    return joined(grad_q), joined(grad_k), joined(grad_v), grad_short, grad_medium
```

```python
import numpy as np
import jax
import jax.numpy as jnp
from jax import lax
from jax.experimental import pallas as pl
from jax.experimental.pallas import tpu as pltpu
from jax.sharding import PartitionSpec as P

HALO = 8
BLOCK = 128
WINDOW = 2 * BLOCK
F32 = jnp.float32
BF16 = jnp.bfloat16


def split_terms(matrix):
    high = matrix.astype(BF16)
    low = (matrix - high.astype(np.float32)).astype(BF16)
    return np.asarray(high), np.asarray(low)


def transforms():
    time = np.arange(WINDOW)
    freq = np.arange(BLOCK)
    angle = 2 * np.pi * ((freq[:, None] * time[None, :]) % WINDOW) / WINDOW
    cosine, sine = np.cos(angle), np.sin(angle)
    nyquist = np.where(time % 2 == 0, 1.0, -1.0)
    forward = np.concatenate([cosine, -sine]).astype(np.float64)
    forward[BLOCK] = nyquist
    scale = np.full(WINDOW, 2.0 / WINDOW)
    scale[0] = scale[BLOCK] = 1.0 / WINDOW
    inverse = forward.T * scale[None, :]
    f_high, f_low = split_terms(forward.astype(np.float32))
    i_high, i_low = split_terms(inverse.astype(np.float32))
    whole = np.concatenate([f_high, f_low], axis=1)
    half = np.concatenate([f_high[:, :BLOCK], f_low[:, :BLOCK]], axis=1)
    back = np.concatenate([i_high, i_high, i_low], axis=1)
    return whole, half, back[:BLOCK], back[BLOCK:]


def dot(left, right):
    return jnp.dot(left, right, preferred_element_type=F32)


def to_spectrum(matrix, rows):
    return dot(matrix, jnp.concatenate([rows, rows], axis=0))


def from_spectrum(matrix, real, imag):
    whole = jnp.concatenate([real, imag], axis=0)
    high = whole.astype(BF16)
    low = (whole - high.astype(F32)).astype(BF16)
    return dot(matrix, jnp.concatenate([high, low, high], axis=0))


def times(spec, taps):
    xr, xi = spec[:BLOCK], spec[BLOCK:]
    return xr * taps[0] - xi * taps[1], xr * taps[1] + xi * taps[2]


def times_conj(spec, taps):
    xr, xi = spec[:BLOCK], spec[BLOCK:]
    return xr * taps[0] + xi * taps[1], xi * taps[2] - xr * taps[1]


def rounded(value):
    return value.astype(BF16).astype(F32)


def lanes_of(width):
    return [slice(at, at + 128) for at in range(0, width, 128)]


def causal(ref, weights, index, count, lanes):
    total = None
    for j in range(weights.shape[1]):
        term = weights[index, j : j + 1, lanes] * ref[pl.ds(HALO - j, count), lanes]
        total = term if total is None else total + term
    return total


def anticausal(ref, weights, index, count, lanes):
    total = None
    for j in range(weights.shape[1]):
        term = weights[index, j : j + 1, lanes] * ref[pl.ds(j, count), lanes]
        total = term if total is None else total + term
    return total


def lag_sums(gradient, ref, taps, lanes):
    count = gradient.shape[0]
    rows = []
    for j in range(taps):
        prod = gradient * ref[pl.ds(HALO - j, count), lanes]
        rows.append(jnp.sum(prod, axis=0, keepdims=True))
    rows.append(jnp.zeros_like(rows[0]))
    return jnp.concatenate(rows, axis=0)


def first_kernel(q, k, v, g, w, tails, heads, ahead, xq):
    rows = q.shape[0]
    low = rows - 2 * HALO
    tails[...] = jnp.concatenate(
        [x[low:, :].astype(F32)[HALO:] for x in (q, k, v)], axis=0
    ).astype(BF16)
    heads[...] = jnp.concatenate(
        [x[: 2 * HALO, :].astype(F32)[:HALO] for x in (q, k, v, g)], axis=0
    ).astype(BF16)
    need = BLOCK + 2 * HALO
    xq[...] = q[:need, :].astype(F32)
    grad = g[:need, :].astype(F32)[HALO : HALO + BLOCK]
    for lanes in lanes_of(q.shape[1]):
        ahead[:, lanes] = (grad[:, lanes] * causal(xq, w, 0, BLOCK, lanes)).astype(BF16)


def second_kernel(
    q, k, v, g, tails, heads, w, taps, half, whole, low, high,
    gated_out, ggi_out, ks_out, vs_out, inner_out, behind_out, spec_out,
    xq, xk, xv, tap_spec,
):
    rows, width = q.shape
    ext = rows + HALO

    @pl.when(pl.program_id(0) == 0)
    def _():
        both = jnp.concatenate([taps[...], taps[...]], axis=1)
        spec = lax.dot_general(half[...], both, (((1,), (1,)), ((), ())), preferred_element_type=F32)
        real, imag = spec[:BLOCK], spec[BLOCK:]
        first = lax.broadcasted_iota(jnp.int32, real.shape, 0) == 0
        tap_spec[0] = real
        tap_spec[1] = jnp.where(first, 0.0, imag)
        tap_spec[2] = jnp.where(first, imag, real)
        spec_out[...] = tap_spec[...]

    tail = tails[...].astype(F32)
    head = heads[...].astype(F32)
    for at, (ref, x) in enumerate(((xq, q), (xk, k), (xv, v))):
        ref[:HALO] = tail[at * HALO : (at + 1) * HALO]
        ref[HALO : HALO + rows] = x[...].astype(F32)
        ref[HALO + rows :] = head[at * HALO : (at + 1) * HALO]
    grad = jnp.concatenate([g[...].astype(F32), head[3 * HALO :]], axis=0)
    gated = []
    for lanes in lanes_of(width):
        ks = causal(xk, w, 1, ext, lanes)
        vs = causal(xv, w, 2, ext, lanes)
        ks_out[:ext, lanes] = ks
        vs_out[:ext, lanes] = vs
        gated.append(ks * vs)
        qs = causal(xq, w, 0, ext, lanes)
        ggi_out[:, lanes] = grad[:, lanes] * qs
    gated = jnp.concatenate(gated, axis=1)
    pad = jnp.zeros((WINDOW - ext, width), F32)
    window = jnp.concatenate([gated, pad], axis=0).astype(BF16)
    gated_out[...] = window[: gated_out.shape[0]]
    behind_out[...] = window[rows - BLOCK : rows]
    first = to_spectrum(half[...], window[:BLOCK])
    inner_out[:BLOCK] = from_spectrum(low[...], *times(first, tap_spec))
    second = to_spectrum(whole[...], window)
    inner_out[BLOCK:] = from_spectrum(high[: ext - BLOCK, :], *times(second, tap_spec))


def third_kernel(
    k, v, tails, gated, ggi, ahead, ks, vs, w, spec, half, whole, low,
    gk_out, gv_out, sums_out, medium_out,
    xk, xv, yk, yv, acc,
):
    rows, width = k.shape
    ext = rows + HALO
    step = pl.program_id(0)

    @pl.when(step == 0)
    def _():
        acc[...] = jnp.zeros_like(acc)

    tail = tails[...].astype(F32)
    for at, (ref, x) in enumerate(((xk, k), (xv, v))):
        ref[:HALO] = tail[(at + 1) * HALO : (at + 2) * HALO]
        ref[HALO:] = x[...].astype(F32)
    pad = jnp.zeros((3 * BLOCK - ext - BLOCK, width), F32)
    ggi_ext = jnp.concatenate([ggi[...], ahead[...].astype(F32), pad], axis=0).astype(BF16)
    own = gated[: WINDOW - BLOCK + 0, :]
    rest = jnp.concatenate(
        [gated[BLOCK:rows, :], jnp.zeros((WINDOW - rows, width), BF16)], axis=0
    )
    parts = []
    for at, mine in ((0, own), (1, rest)):
        win = to_spectrum(whole[...], ggi_ext[at * BLOCK : at * BLOCK + WINDOW])
        gs = to_spectrum(half[...], mine)
        acc[0] += gs[:BLOCK] * win[:BLOCK]
        acc[1] += gs[BLOCK:] * win[BLOCK:]
        acc[2] += gs[:BLOCK] * win[BLOCK:] - gs[BLOCK:] * win[:BLOCK]
        count = min(BLOCK, ext - at * BLOCK)
        parts.append(from_spectrum(low[:count, :], *times_conj(win, spec)))
    gg = jnp.concatenate(parts, axis=0)
    yk[:ext] = rounded(gg * vs[:ext, :])
    yv[:ext] = rounded(gg * ks[:ext, :])
    for lanes in lanes_of(width):
        gk_out[:, lanes] = anticausal(yk, w, 1, rows, lanes).astype(BF16)
        gv_out[:, lanes] = anticausal(yv, w, 2, rows, lanes).astype(BF16)
        sums_out[:HALO, lanes] = lag_sums(yk[:rows, lanes], xk, w.shape[1], lanes)
        sums_out[HALO:, lanes] = lag_sums(yv[:rows, lanes], xv, w.shape[1], lanes)

    @pl.when(step == pl.num_programs(0) - 1)
    def _():
        first = lax.broadcasted_iota(jnp.int32, (BLOCK, width), 0) == 0
        real = acc[0] + jnp.where(first, 0.0, acc[1])
        imag = jnp.where(first, acc[1], acc[2])
        medium_out[...] = from_spectrum(low[...], real, imag).T


def fourth_kernel(
    q, g, tails, heads, inner, behind, w, spec, half, high,
    gq_out, sums_out,
    xq, yq,
):
    rows, width = q.shape
    ext = rows + HALO
    xq[:HALO] = tails[...].astype(F32)[:HALO]
    xq[HALO:] = q[...].astype(F32)
    edge = from_spectrum(high[...], *times(to_spectrum(half[...], behind[...]), spec))
    yq[:BLOCK] = rounded(g[:BLOCK, :].astype(F32) * (inner[:BLOCK, :] + edge))
    yq[BLOCK:rows] = rounded(g[BLOCK:, :].astype(F32) * inner[BLOCK:rows, :])
    yq[rows:ext] = rounded(heads[...].astype(F32)[3 * HALO :] * inner[rows:ext, :])
    for lanes in lanes_of(width):
        gq_out[:, lanes] = anticausal(yq, w, 0, rows, lanes).astype(BF16)
        sums_out[:, lanes] = lag_sums(yq[:rows, lanes], xq, w.shape[1], lanes)


def shift(value, axis, steps):
    count = lax.axis_size(axis)
    initial, last = (max(0, -steps), min(count, count - steps))
    return lax.ppermute(value, axis, [(s, s + steps) for s in range(initial, last)])


def gather_rows(value, axis):
    count, rows = lax.axis_size(axis), value.shape[0]
    me = lax.axis_index(axis)
    result = jnp.zeros((count * rows, value.shape[1]), value.dtype)
    result = lax.dynamic_update_slice(result, value, (me * rows, 0))
    for step in range(1, count):
        other = lax.ppermute(value, axis, [(s, (s + step) % count) for s in range(count)])
        result = lax.dynamic_update_slice(result, other, ((me - step) % count * rows, 0))
    return result


def scatter_sum(value, axis):
    count = lax.axis_size(axis)
    rows = value.shape[0] // count
    me = lax.axis_index(axis)
    total = lax.dynamic_slice(value, (me * rows, 0), (rows, value.shape[1]))
    for step in range(1, count):
        part = lax.dynamic_slice(value, ((me + step) % count * rows, 0), (rows, value.shape[1]))
        total = total + lax.ppermute(
            part.astype(BF16), axis, [(s, (s + step) % count) for s in range(count)]
        ).astype(F32)
    return total


def sum_over(value, axis):
    count = lax.axis_size(axis)
    if count & (count - 1):
        return lax.psum(value, axis)
    distance = 1
    while distance < count:
        other = lax.ppermute(value.astype(BF16), axis, [(s, s ^ distance) for s in range(count)])
        value = value + other.astype(F32)
        distance *= 2
    return value


def shards(query, key, value, grad_out, short_filter, medium_filter):
    rows, channels = query.shape
    groups = medium_filter.shape[0] * lax.axis_size("fsdp")
    width, tiles = groups, channels // groups
    ext = rows + HALO
    pad_rows = rows + 2 * HALO
    taps_short = short_filter.shape[1]
    whole, half, low, high = (jnp.asarray(m) for m in transforms())

    def col(count):
        return pl.BlockSpec((count, width), lambda i: (0, i))

    def fixed(shape):
        return pl.BlockSpec(shape, lambda i: (0,) * len(shape))

    weights = pl.BlockSpec((3, taps_short, width), lambda i: (0, 0, i))

    def out(count, dtype):
        return jax.ShapeDtypeStruct((count, channels), dtype)

    params = pltpu.CompilerParams(vmem_limit_bytes=48 * 1024 * 1024)

    def cost(flops, moved):
        return pl.CostEstimate(flops=int(flops), bytes_accessed=int(moved), transcendentals=0)

    tails, heads, ahead = pl.pallas_call(
        first_kernel,
        grid=(tiles,),
        in_specs=[col(rows)] * 4 + [weights],
        out_specs=[col(3 * HALO), col(4 * HALO), col(BLOCK)],
        out_shape=[out(3 * HALO, BF16), out(4 * HALO, BF16), out(BLOCK, BF16)],
        scratch_shapes=[pltpu.VMEM((BLOCK + 2 * HALO, width), F32)],
        compiler_params=params,
        name="first",
    )(query, key, value, grad_out, short_filter)
    taps = gather_rows(medium_filter.astype(BF16), "fsdp")
    tails = shift(tails, "seq", 1)
    heads = shift(heads, "seq", -1)
    ahead = shift(ahead, "seq", -1)

    gated, ggi, ks, vs, inner, behind, spec = pl.pallas_call(
        second_kernel,
        grid=(tiles,),
        in_specs=[col(rows)] * 4
        + [col(3 * HALO), col(4 * HALO), weights, fixed(taps.shape)]
        + [fixed(m.shape) for m in (half, whole, low, high)],
        out_specs=[col(pad_rows), col(ext), col(ext), col(ext), col(ext), col(BLOCK), fixed((3, BLOCK, width))],
        out_shape=[
            out(pad_rows, BF16), out(ext, F32), out(ext, F32), out(ext, F32), out(ext, F32),
            out(BLOCK, BF16), jax.ShapeDtypeStruct((3, BLOCK, width), F32),
        ],
        scratch_shapes=[pltpu.VMEM((rows + 2 * HALO, width), F32)] * 3
        + [pltpu.VMEM((3, BLOCK, width), F32)],
        compiler_params=params,
        cost_estimate=cost(2e9, 12e6),
        name="second",
    )(query, key, value, grad_out, tails, heads, short_filter, taps, half, whole, low, high)
    behind = shift(behind, "seq", 1)

    grad_key, grad_value, sums_kv, medium = pl.pallas_call(
        third_kernel,
        grid=(tiles,),
        in_specs=[col(rows)] * 2
        + [col(3 * HALO), col(pad_rows), col(ext), col(BLOCK), col(ext), col(ext), weights]
        + [fixed((3, BLOCK, width))]
        + [fixed(m.shape) for m in (half, whole, low)],
        out_specs=[col(rows), col(rows), col(2 * HALO), fixed((width, BLOCK))],
        out_shape=[out(rows, BF16), out(rows, BF16), out(2 * HALO, F32), jax.ShapeDtypeStruct((width, BLOCK), F32)],
        scratch_shapes=[pltpu.VMEM((rows + HALO, width), F32)] * 4
        + [pltpu.VMEM((3, BLOCK, width), F32)],
        compiler_params=params,
        cost_estimate=cost(4e9, 12e6),
        name="third",
    )(key, value, tails, gated, ggi, ahead, ks, vs, short_filter, spec, half, whole, low)

    grad_query, sums_q = pl.pallas_call(
        fourth_kernel,
        grid=(tiles,),
        in_specs=[col(rows)] * 2
        + [col(3 * HALO), col(4 * HALO), col(ext), col(BLOCK), weights]
        + [fixed((3, BLOCK, width))]
        + [fixed(m.shape) for m in (half, high)],
        out_specs=[col(rows), col(HALO)],
        out_shape=[out(rows, BF16), out(HALO, F32)],
        scratch_shapes=[pltpu.VMEM((rows + HALO, width), F32)] * 2,
        compiler_params=params,
        cost_estimate=cost(1e9, 6e6),
        name="fourth",
    )(query, grad_out, tails, heads, inner, behind, short_filter, spec, half, high)

    medium = scatter_sum(medium, "fsdp")
    per = channels // BLOCK
    count = medium.shape[0] // per
    packed = jnp.concatenate([medium[i * count : (i + 1) * count] for i in range(per)], axis=1)
    late = sum_over(jnp.concatenate([sums_kv, packed], axis=0), "seq")
    sums_q = sum_over(sums_q, "seq")
    packed = late[2 * HALO :]
    grad_medium = jnp.concatenate([packed[:, i * BLOCK : (i + 1) * BLOCK] for i in range(per)], axis=0)
    grad_short = jnp.stack([sums_q[:taps_short], late[:taps_short], late[HALO : HALO + taps_short]])
    return grad_query, grad_key, grad_value, grad_short, grad_medium


def solution(mesh):
    in_specs = (
        P("seq", "fsdp"),
        P("seq", "fsdp"),
        P("seq", "fsdp"),
        P("seq", "fsdp"),
        P(None, None, "fsdp"),
        P("fsdp", None),
    )
    out_specs = (
        P("seq", "fsdp"),
        P("seq", "fsdp"),
        P("seq", "fsdp"),
        P(None, None, "fsdp"),
        P("fsdp", None),
    )
    return jax.shard_map(shards, mesh=mesh, in_specs=in_specs, out_specs=out_specs, check_vma=False)
```

```python
import numpy as np
import jax
import jax.numpy as jnp
from jax import lax
from jax.experimental import pallas as pl
from jax.experimental.pallas import tpu as pltpu
from jax.sharding import PartitionSpec as P


HALO = 8
BLOCK = 128
WINDOW = 2 * BLOCK
F32 = jnp.float32
BF16 = jnp.bfloat16


def split_terms(matrix):
    high = matrix.astype(BF16)
    low = (matrix - high.astype(np.float32)).astype(BF16)
    return np.asarray(high), np.asarray(low)


def transforms():
    time = np.arange(WINDOW)
    freq = np.arange(BLOCK)
    angle = 2 * np.pi * ((freq[:, None] * time[None, :]) % WINDOW) / WINDOW
    cosine, sine = np.cos(angle), np.sin(angle)
    nyquist = np.where(time % 2 == 0, 1.0, -1.0)
    forward = np.concatenate([cosine, -sine]).astype(np.float64)
    forward[BLOCK] = nyquist
    scale = np.full(WINDOW, 2.0 / WINDOW)
    scale[0] = scale[BLOCK] = 1.0 / WINDOW
    inverse = forward.T * scale[None, :]
    f_high, f_low = split_terms(forward.astype(np.float32))
    i_high, i_low = split_terms(inverse.astype(np.float32))
    whole = np.concatenate([f_high, f_low], axis=1)
    half = np.concatenate([f_high[:, :BLOCK], f_low[:, :BLOCK]], axis=1)
    back = np.concatenate([i_high, i_low], axis=1)
    return whole, half, back[:BLOCK], back[BLOCK:]


def dot(left, right):
    return jnp.dot(left, right, preferred_element_type=F32)


def to_spectrum(matrix, rows):
    return dot(matrix, jnp.concatenate([rows, rows], axis=0))


def from_spectrum(matrix, real, imag):
    whole = jnp.concatenate([real, imag], axis=0).astype(BF16)
    return to_spectrum(matrix, whole)


def times(spec, taps):
    xr, xi = spec[:BLOCK], spec[BLOCK:]
    return xr * taps[0] - xi * taps[1], xr * taps[1] + xi * taps[2]


def times_conj(spec, taps):
    xr, xi = spec[:BLOCK], spec[BLOCK:]
    return xr * taps[0] + xi * taps[1], xi * taps[2] - xr * taps[1]


def rounded(value):
    return value.astype(BF16).astype(F32)


LANES = 128
CHUNK = 64


def halves(width):
    return [(at // LANES, slice(at, at + LANES)) for at in range(0, width, LANES)]


def pieces(count):
    return [(at, min(CHUNK, count - at)) for at in range(0, count, CHUNK)]


def put(ref, at, value):
    for h, lanes in halves(value.shape[1]):
        ref[h, at : at + value.shape[0]] = value[:, lanes]


def causal(ref, h, at, count, weights):
    total = None
    for j, weight in enumerate(weights):
        term = weight * ref[h, at - j : at - j + count]
        total = term if total is None else total + term
    return total


def anticausal(ref, h, at, count, weights):
    total = None
    for j, weight in enumerate(weights):
        term = weight * ref[h, at + j : at + j + count]
        total = term if total is None else total + term
    return total


def taps_of(w, index, lanes):
    return [w[index, j : j + 1, lanes] for j in range(w.shape[1])]


def lag_sums(grad, g_at, x, x_at, h, count, taps):
    totals = [None] * taps
    for at, size in pieces(count):
        mine = grad[h, g_at + at : g_at + at + size]
        for j in range(taps):
            prod = mine * x[h, x_at + at - j : x_at + at - j + size]
            part = jnp.sum(prod.reshape(size // 8, 8, LANES), axis=0)
            totals[j] = part if totals[j] is None else totals[j] + part
    rows = [jnp.sum(t, axis=0, keepdims=True) for t in totals]
    return jnp.concatenate(rows + [jnp.zeros_like(rows[0])], axis=0)


def first_kernel(q, g, q_tail, k_tail, v_tail, k_head, v_head, w, tails, ahead, xq):
    tails[...] = jnp.concatenate(
        [x[...].astype(F32)[HALO:] for x in (q_tail, k_tail, v_tail)], axis=0
    ).astype(BF16)
    put(xq, 0, q[...].astype(F32))
    grad = g[...].astype(F32)
    heads = [x[: 2 * HALO, :].astype(F32)[:HALO] for x in (q, k_head, v_head, g)]
    ahead[: 4 * HALO] = jnp.concatenate(heads, axis=0).astype(BF16)
    for h, lanes in halves(q.shape[1]):
        weights = taps_of(w, 0, lanes)
        for at, size in pieces(BLOCK):
            qs = causal(xq, h, HALO + at, size, weights)
            ahead[4 * HALO + at : 4 * HALO + at + size, lanes] = (
                grad[HALO + at : HALO + at + size, lanes] * qs
            ).astype(BF16)


def second_kernel(
    q, k, v, g, tails, w, taps, half, low,
    gated_out, ggi_out, ks_out, vs_out, inner_out, behind_out, spec_out,
    xq, xk, xv, tap_spec,
):
    rows, width = q.shape

    @pl.when(pl.program_id(0) == 0)
    def _():
        both = jnp.concatenate([taps[...], taps[...]], axis=1)
        spec = lax.dot_general(half[...], both, (((1,), (1,)), ((), ())), preferred_element_type=F32)
        real, imag = spec[:BLOCK], spec[BLOCK:]
        first = lax.broadcasted_iota(jnp.int32, real.shape, 0) == 0
        tap_spec[0] = real
        tap_spec[1] = jnp.where(first, 0.0, imag)
        tap_spec[2] = jnp.where(first, imag, real)
        spec_out[...] = tap_spec[...]

    tail = tails[...].astype(F32)
    for at, (ref, x) in enumerate(((xq, q), (xk, k), (xv, v))):
        put(ref, 0, tail[at * HALO : (at + 1) * HALO])
        put(ref, HALO, x[...].astype(F32))
    for h, lanes in halves(width):
        wq, wk, wv = (taps_of(w, i, lanes) for i in range(3))
        for at, size in pieces(rows):
            span = slice(at, at + size)
            ks = causal(xk, h, HALO + at, size, wk)
            vs = causal(xv, h, HALO + at, size, wv)
            ks_out[span, lanes] = ks
            vs_out[span, lanes] = vs
            gated_out[span, lanes] = (ks * vs).astype(BF16)
            qs = causal(xq, h, HALO + at, size, wq)
            ggi_out[span, lanes] = (g[span, lanes].astype(F32) * qs).astype(BF16)
    behind_out[...] = gated_out[rows - BLOCK :, :]
    first = to_spectrum(half[...], gated_out[:BLOCK, :])
    inner_out[...] = from_spectrum(low[...], *times(first, tap_spec))


def third_kernel(
    q, k, v, g, tails, ahead, gated, ggi, ks, vs, w, spec, half, whole, low, high,
    gk_out, gv_out, gq_out, next_out, sums_out, medium_out,
    xq, xk, xv, yq, yk, yv, acc,
):
    rows, width = k.shape
    rest = rows - BLOCK
    step = pl.program_id(0)
    count = w.shape[1]

    @pl.when(step == 0)
    def _():
        acc[...] = jnp.zeros_like(acc)

    tail = tails[...].astype(F32)
    head = ahead[: 4 * HALO, :].astype(F32)
    for at, (ref, x) in enumerate(((xq, q), (xk, k), (xv, v))):
        put(ref, 0, tail[at * HALO : (at + 1) * HALO])
        put(ref, HALO, x[...].astype(F32))
        put(ref, HALO + rows, head[at * HALO : (at + 1) * HALO])
    gated_new, ggi_new, ks_new, vs_new = [], [], [], []
    for h, lanes in halves(width):
        kn, vn, qn = (
            causal(ref, h, HALO + rows, HALO, taps_of(w, i, lanes))
            for ref, i in ((xk, 1), (xv, 2), (xq, 0))
        )
        ks_new.append(kn)
        vs_new.append(vn)
        gated_new.append(kn * vn)
        ggi_new.append(head[3 * HALO :, lanes] * qn)
    ks_new, vs_new, gated_new, ggi_new = (
        jnp.concatenate(x, axis=1) for x in (ks_new, vs_new, gated_new, ggi_new)
    )
    blank = jnp.zeros((WINDOW - rows - HALO, width), F32)
    rest_new = jnp.concatenate([gated_new, blank], axis=0).astype(BF16)
    window = jnp.concatenate([gated[...], rest_new], axis=0)
    sig = from_spectrum(high[: rest + HALO, :], *times(to_spectrum(whole[...], window), spec))
    put(yq, 0, rounded(g[BLOCK:, :].astype(F32) * sig[:rest]))
    put(yq, rest, rounded(head[3 * HALO :] * sig[rest:]))
    for h, lanes in halves(width):
        next_out[:, lanes] = yq[h, :HALO]

    fill = 3 * BLOCK - rows - HALO - BLOCK
    later = jnp.concatenate(
        [ggi_new, ahead[4 * HALO :, :].astype(F32), jnp.zeros((fill, width), F32)], axis=0
    ).astype(BF16)
    ggi_ext = jnp.concatenate([ggi[...], later], axis=0)
    own = jnp.concatenate([gated[...], jnp.zeros((WINDOW - rows, width), BF16)], axis=0)
    for at in range(2):
        win = to_spectrum(whole[...], ggi_ext[at * BLOCK : at * BLOCK + WINDOW])
        gs = to_spectrum(half[...], own[at * BLOCK : (at + 1) * BLOCK])
        acc[0] += gs[:BLOCK] * win[:BLOCK]
        acc[1] += gs[BLOCK:] * win[BLOCK:]
        acc[2] += gs[:BLOCK] * win[BLOCK:] - gs[BLOCK:] * win[:BLOCK]
        prod = times_conj(win, spec)
        if at == 0:
            gg = from_spectrum(low[...], *prod)
            put(yk, 0, rounded(gg * vs[:BLOCK, :]))
            put(yv, 0, rounded(gg * ks[:BLOCK, :]))
        else:
            gg = from_spectrum(low[: rest + HALO, :], *prod)
            put(yk, BLOCK, rounded(gg[:rest] * vs[BLOCK:, :]))
            put(yv, BLOCK, rounded(gg[:rest] * ks[BLOCK:, :]))
            put(yk, rows, rounded(gg[rest:] * vs_new))
            put(yv, rows, rounded(gg[rest:] * ks_new))
    for h, lanes in halves(width):
        for i, ref, out in ((1, yk, gk_out), (2, yv, gv_out)):
            weights = taps_of(w, i, lanes)
            for at, size in pieces(rows):
                out[at : at + size, lanes] = anticausal(ref, h, at, size, weights).astype(BF16)
        gq_out[:, lanes] = anticausal(yq, h, 0, rest, taps_of(w, 0, lanes)).astype(BF16)
        sums_out[:HALO, lanes] = lag_sums(yk, 0, xk, HALO, h, rows, count)
        sums_out[HALO : 2 * HALO, lanes] = lag_sums(yv, 0, xv, HALO, h, rows, count)
        sums_out[2 * HALO :, lanes] = lag_sums(yq, 0, xq, HALO + BLOCK, h, rest, count)

    @pl.when(step == pl.num_programs(0) - 1)
    def _():
        first = lax.broadcasted_iota(jnp.int32, (BLOCK, width), 0) == 0
        real = acc[0] + jnp.where(first, 0.0, acc[1])
        imag = jnp.where(first, acc[1], acc[2])
        medium_out[...] = from_spectrum(low[...], real, imag).T


def fourth_kernel(
    q, g, tails, inner, behind, following, sums, w, spec, half, high, gq_in,
    gq_out, sums_out,
    xq, yq,
):
    width = q.shape[1]
    put(xq, 0, tails[...].astype(F32)[:HALO])
    put(xq, HALO, q[...].astype(F32))
    edge = from_spectrum(high[...], *times(to_spectrum(half[...], behind[...]), spec))
    put(yq, 0, rounded(g[...].astype(F32) * (inner[...] + edge)))
    put(yq, BLOCK, following[...])
    for h, lanes in halves(width):
        weights = taps_of(w, 0, lanes)
        for at, size in pieces(BLOCK):
            gq_out[at : at + size, lanes] = anticausal(yq, h, at, size, weights).astype(BF16)
        sums_out[:, lanes] = sums[:, lanes] + lag_sums(yq, 0, xq, HALO, h, BLOCK, w.shape[1])


def shift(value, axis, steps):
    count = lax.axis_size(axis)
    initial, last = (max(0, -steps), min(count, count - steps))
    return lax.ppermute(value, axis, [(s, s + steps) for s in range(initial, last)])


def gather_rows(value, axis):
    count, rows = lax.axis_size(axis), value.shape[0]
    me = lax.axis_index(axis)
    result = jnp.zeros((count * rows, value.shape[1]), value.dtype)
    result = lax.dynamic_update_slice(result, value, (me * rows, 0))
    for step in range(1, count):
        other = lax.ppermute(value, axis, [(s, (s + step) % count) for s in range(count)])
        result = lax.dynamic_update_slice(result, other, ((me - step) % count * rows, 0))
    return result


def scatter_sum(value, axis):
    count = lax.axis_size(axis)
    rows = value.shape[0] // count
    me = lax.axis_index(axis)
    total = lax.dynamic_slice(value, (me * rows, 0), (rows, value.shape[1]))
    for step in range(1, count):
        part = lax.dynamic_slice(value, ((me + step) % count * rows, 0), (rows, value.shape[1]))
        total = total + lax.ppermute(
            part.astype(BF16), axis, [(s, (s + step) % count) for s in range(count)]
        ).astype(F32)
    return total


def sum_over(value, axis):
    count = lax.axis_size(axis)
    if count & (count - 1):
        return lax.psum(value, axis)
    distance = 1
    while distance < count:
        other = lax.ppermute(value.astype(BF16), axis, [(s, s ^ distance) for s in range(count)])
        value = value + other.astype(F32)
        distance *= 2
    return value


def shards(query, key, value, grad_out, short_filter, medium_filter):
    rows, channels = query.shape
    groups = medium_filter.shape[0] * lax.axis_size("fsdp")
    width, tiles = groups, channels // groups
    rest = rows - BLOCK
    taps_short = short_filter.shape[1]
    whole, half, low, high = (jnp.asarray(m) for m in transforms())

    def col(count, at=0, wide=width):
        return pl.BlockSpec((count, wide), lambda i: (at, i))

    def fixed(shape):
        return pl.BlockSpec(shape, lambda i: (0,) * len(shape))

    def filters(wide=width):
        return pl.BlockSpec((3, taps_short, wide), lambda i: (0, 0, i))

    def out(count, dtype):
        return jax.ShapeDtypeStruct((count, channels), dtype)

    def scratch(count, wide=width):
        return pltpu.VMEM((wide // LANES, count, LANES), F32)

    def cost(flops, moved):
        return pl.CostEstimate(flops=int(flops), bytes_accessed=int(moved), transcendentals=0)

    wide = 2 * width
    last = rows // (2 * HALO) - 1
    tails, ahead = pl.pallas_call(
        first_kernel,
        grid=(channels // wide,),
        in_specs=[col(BLOCK + 2 * HALO, 0, wide)] * 2
        + [col(2 * HALO, last, wide)] * 3
        + [col(2 * HALO, 0, wide)] * 2
        + [filters(wide)],
        out_specs=[col(3 * HALO, 0, wide), col(BLOCK + 4 * HALO, 0, wide)],
        out_shape=[out(3 * HALO, BF16), out(BLOCK + 4 * HALO, BF16)],
        scratch_shapes=[scratch(BLOCK + 2 * HALO, wide)],
        name="first",
    )(query, grad_out, query, key, value, key, value, short_filter)
    tails = shift(tails, "seq", 1)
    ahead = shift(ahead, "seq", -1)
    taps = gather_rows(medium_filter.astype(BF16), "fsdp")

    gated, ggi, ks, vs, inner, behind, spec = pl.pallas_call(
        second_kernel,
        grid=(tiles,),
        in_specs=[col(rows)] * 4
        + [col(3 * HALO), filters(), fixed(taps.shape), fixed(half.shape), fixed(low.shape)],
        out_specs=[col(rows)] * 4 + [col(BLOCK), col(BLOCK), fixed((3, BLOCK, width))],
        out_shape=[
            out(rows, BF16), out(rows, BF16), out(rows, F32), out(rows, F32),
            out(BLOCK, F32), out(BLOCK, BF16), jax.ShapeDtypeStruct((3, BLOCK, width), F32),
        ],
        scratch_shapes=[scratch(rows + HALO)] * 3 + [pltpu.VMEM((3, BLOCK, width), F32)],
        cost_estimate=cost(4e9, 20e6),
        name="second",
    )(query, key, value, grad_out, tails, short_filter, taps, half, low)
    behind = shift(behind, "seq", 1)

    grad_key, grad_value, grad_query, following, sums, medium = pl.pallas_call(
        third_kernel,
        grid=(tiles,),
        in_specs=[col(rows)] * 4
        + [col(3 * HALO), col(BLOCK + 4 * HALO)]
        + [col(rows)] * 4
        + [filters(), fixed((3, BLOCK, width))]
        + [fixed(m.shape) for m in (half, whole, low, high)],
        out_specs=[
            col(rows), col(rows), col(rest, BLOCK // rest), col(HALO), col(3 * HALO),
            fixed((width, BLOCK)),
        ],
        out_shape=[
            out(rows, BF16), out(rows, BF16), out(rows, BF16), out(HALO, F32),
            out(3 * HALO, F32), jax.ShapeDtypeStruct((width, BLOCK), F32),
        ],
        scratch_shapes=[scratch(rows + 2 * HALO)] * 3
        + [scratch(rest + 2 * HALO)]
        + [scratch(rows + 2 * HALO)] * 2
        + [pltpu.VMEM((3, BLOCK, width), F32)],
        cost_estimate=cost(8e9, 30e6),
        name="third",
    )(query, key, value, grad_out, tails, ahead, gated, ggi, ks, vs, short_filter, spec,
      half, whole, low, high)

    grad_query, sums_q = pl.pallas_call(
        fourth_kernel,
        grid=(tiles,),
        in_specs=[col(BLOCK)] * 2
        + [col(3 * HALO), col(BLOCK), col(BLOCK), col(HALO), col(HALO, 2), filters()]
        + [fixed((3, BLOCK, width)), fixed(half.shape), fixed(high.shape)]
        + [pl.BlockSpec(memory_space=pl.ANY)],
        out_specs=[col(BLOCK), col(HALO)],
        out_shape=[out(rows, BF16), out(HALO, F32)],
        scratch_shapes=[scratch(BLOCK + HALO)] * 2,
        input_output_aliases={11: 0},
        cost_estimate=cost(2e9, 8e6),
        name="fourth",
    )(query, grad_out, tails, inner, behind, following, sums, short_filter, spec, half, high,
      grad_query)

    medium = scatter_sum(medium, "fsdp")
    per = channels // BLOCK
    count = medium.shape[0] // per
    packed = jnp.concatenate([medium[i * count : (i + 1) * count] for i in range(per)], axis=1)
    early = jnp.concatenate([sums[: 2 * HALO], packed], axis=0)
    early = sum_over(early, "seq")
    sums_q = sum_over(sums_q, "seq")
    packed = early[2 * HALO :]
    grad_medium = jnp.concatenate([packed[:, i * BLOCK : (i + 1) * BLOCK] for i in range(per)], axis=0)
    grad_short = jnp.stack([sums_q[:taps_short], early[:taps_short], early[HALO : HALO + taps_short]])
    return grad_query, grad_key, grad_value, grad_short, grad_medium


def solution(mesh):
    in_specs = (
        P("seq", "fsdp"),
        P("seq", "fsdp"),
        P("seq", "fsdp"),
        P("seq", "fsdp"),
        P(None, None, "fsdp"),
        P("fsdp", None),
    )
    out_specs = (
        P("seq", "fsdp"),
        P("seq", "fsdp"),
        P("seq", "fsdp"),
        P(None, None, "fsdp"),
        P("fsdp", None),
    )
    return jax.shard_map(shards, mesh=mesh, in_specs=in_specs, out_specs=out_specs, check_vma=False)
```

```python
import numpy as np
import jax
import jax.numpy as jnp
from jax import lax
from jax.experimental import pallas as pl
from jax.experimental.pallas import tpu as pltpu
from jax.sharding import PartitionSpec as P


HALO = 8
BLOCK = 128
WINDOW = 2 * BLOCK
F32 = jnp.float32
BF16 = jnp.bfloat16


def split_terms(matrix):
    high = matrix.astype(BF16)
    low = (matrix - high.astype(np.float32)).astype(BF16)
    return np.asarray(high), np.asarray(low)


def transforms():
    time = np.arange(WINDOW)
    freq = np.arange(BLOCK)
    angle = 2 * np.pi * ((freq[:, None] * time[None, :]) % WINDOW) / WINDOW
    cosine, sine = np.cos(angle), np.sin(angle)
    nyquist = np.where(time % 2 == 0, 1.0, -1.0)
    forward = np.concatenate([cosine, -sine]).astype(np.float64)
    forward[BLOCK] = nyquist
    scale = np.full(WINDOW, 2.0 / WINDOW)
    scale[0] = scale[BLOCK] = 1.0 / WINDOW
    inverse = forward.T * scale[None, :]
    f_high, f_low = split_terms(forward.astype(np.float32))
    i_high, i_low = split_terms(inverse.astype(np.float32))
    whole = np.concatenate([f_high, f_low], axis=1)
    half = np.concatenate([f_high[:, :BLOCK], f_low[:, :BLOCK]], axis=1)
    back = np.concatenate([i_high, i_low], axis=1)
    return whole, half, back[:BLOCK], back[BLOCK:]


def dot(left, right):
    return jnp.dot(left, right, preferred_element_type=F32)


def to_spectrum(matrix, rows):
    return dot(matrix, jnp.concatenate([rows, rows], axis=0))


def from_spectrum(matrix, real, imag):
    whole = jnp.concatenate([real, imag], axis=0).astype(BF16)
    return to_spectrum(matrix, whole)


def times(spec, taps):
    xr, xi = spec[:BLOCK], spec[BLOCK:]
    return xr * taps[0] - xi * taps[1], xr * taps[1] + xi * taps[2]


def times_conj(spec, taps):
    xr, xi = spec[:BLOCK], spec[BLOCK:]
    return xr * taps[0] + xi * taps[1], xi * taps[2] - xr * taps[1]


def blocks(wide, width):
    return [slice(at, at + width) for at in range(0, wide, width)]


def rounded(value):
    return value.astype(BF16).astype(F32)


LANES = 128
CHUNK = 64


def halves(width):
    return [(at // LANES, slice(at, at + LANES)) for at in range(0, width, LANES)]


def pieces(count):
    return [(at, min(CHUNK, count - at)) for at in range(0, count, CHUNK)]


def put(ref, at, value, lane=0):
    for h, lanes in halves(value.shape[1]):
        ref[h + lane // LANES, at : at + value.shape[0]] = value[:, lanes]


def causal(ref, h, at, count, weights):
    total = None
    for j, weight in enumerate(weights):
        term = weight * ref[h, at - j : at - j + count]
        total = term if total is None else total + term
    return total


def anticausal(ref, h, at, count, weights):
    total = None
    for j, weight in enumerate(weights):
        term = weight * ref[h, at + j : at + j + count]
        total = term if total is None else total + term
    return total


def taps_of(w, index, lanes):
    return [w[index, j : j + 1, lanes] for j in range(w.shape[1])]


def lag_sums(grad, g_at, x, x_at, h, count, taps):
    totals = [None] * taps
    for at, size in pieces(count):
        mine = grad[h, g_at + at : g_at + at + size]
        for j in range(taps):
            prod = mine * x[h, x_at + at - j : x_at + at - j + size]
            part = jnp.sum(prod.reshape(size // 8, 8, LANES), axis=0)
            totals[j] = part if totals[j] is None else totals[j] + part
    rows = [jnp.sum(t, axis=0, keepdims=True) for t in totals]
    return jnp.concatenate(rows + [jnp.zeros_like(rows[0])], axis=0)


def first_kernel(q, g, q_tail, k_tail, v_tail, k_head, v_head, w, tails, ahead, xq):
    tails[...] = jnp.concatenate(
        [x[...].astype(F32)[HALO:] for x in (q_tail, k_tail, v_tail)], axis=0
    ).astype(BF16)
    put(xq, 0, q[...].astype(F32))
    grad = g[...].astype(F32)
    heads = [x[: 2 * HALO, :].astype(F32)[:HALO] for x in (q, k_head, v_head, g)]
    ahead[: 4 * HALO] = jnp.concatenate(heads, axis=0).astype(BF16)
    for h, lanes in halves(q.shape[1]):
        weights = taps_of(w, 0, lanes)
        for at, size in pieces(BLOCK):
            qs = causal(xq, h, HALO + at, size, weights)
            ahead[4 * HALO + at : 4 * HALO + at + size, lanes] = (
                grad[HALO + at : HALO + at + size, lanes] * qs
            ).astype(BF16)


def second_kernel(
    q, k, v, g, tails, w, taps, half, low,
    gated_out, ggi_out, ks_out, vs_out, inner_out, behind_out, spec_out,
    xq, xk, xv, tap_spec,
):
    rows, width = q.shape

    @pl.when(pl.program_id(0) == 0)
    def _():
        both = jnp.concatenate([taps[...], taps[...]], axis=1)
        spec = lax.dot_general(half[...], both, (((1,), (1,)), ((), ())), preferred_element_type=F32)
        real, imag = spec[:BLOCK], spec[BLOCK:]
        first = lax.broadcasted_iota(jnp.int32, real.shape, 0) == 0
        tap_spec[0] = real
        tap_spec[1] = jnp.where(first, 0.0, imag)
        tap_spec[2] = jnp.where(first, imag, real)
        spec_out[...] = tap_spec[...]

    tail = tails[...].astype(F32)
    for at, (ref, x) in enumerate(((xq, q), (xk, k), (xv, v))):
        put(ref, 0, tail[at * HALO : (at + 1) * HALO])
        put(ref, HALO, x[...].astype(F32))
    for h, lanes in halves(width):
        wq, wk, wv = (taps_of(w, i, lanes) for i in range(3))
        for at, size in pieces(rows):
            span = slice(at, at + size)
            ks = causal(xk, h, HALO + at, size, wk)
            vs = causal(xv, h, HALO + at, size, wv)
            ks_out[span, lanes] = ks
            vs_out[span, lanes] = vs
            gated_out[span, lanes] = (ks * vs).astype(BF16)
            qs = causal(xq, h, HALO + at, size, wq)
            ggi_out[span, lanes] = (g[span, lanes].astype(F32) * qs).astype(BF16)
    behind_out[...] = gated_out[rows - BLOCK :, :]
    for lanes in blocks(width, taps.shape[0]):
        first = to_spectrum(half[...], gated_out[:BLOCK, lanes])
        inner_out[:, lanes] = from_spectrum(low[...], *times(first, tap_spec))


def middle_kernel(
    q, g, gated, w, spec, whole, high,
    gq_out, next_out, sums_out, more_out,
    xq, yq,
):
    rows, width = gated.shape
    rest = rows - BLOCK
    for lanes in blocks(width, spec.shape[2]):
        wide = lanes.stop - lanes.start
        window = jnp.concatenate(
            [gated[:, lanes], jnp.zeros((WINDOW - rows, wide), BF16)], axis=0
        )
        prod = times(to_spectrum(whole[...], window), spec)
        sig = from_spectrum(high[: rest + HALO, :], *prod)
        put(yq, 0, rounded(g[:, lanes].astype(F32) * sig[:rest]), lanes.start)
        more_out[:, lanes] = sig[rest:]
    put(xq, 0, q[BLOCK - 2 * HALO :, :].astype(F32))
    for h, lanes in halves(width):
        next_out[:HALO, lanes] = yq[h, :HALO]
        next_out[HALO:, lanes] = yq[h, rest - HALO : rest]
        gq_out[:, lanes] = anticausal(yq, h, 0, rest, taps_of(w, 0, lanes)).astype(BF16)
        sums_out[:, lanes] = lag_sums(yq, 0, xq, 2 * HALO, h, rest, w.shape[1])


def third_kernel(
    me, k, v, tails, ends, ahead, gated, ggi, ks, vs, more, taps, w, spec, half, whole, low,
    gk_out, gv_out, next_out, sums_out, send_out, own_out, *rest_refs,
):
    *more_out, xe, xk, xv, yk, yv, acc, mscr = rest_refs
    rows, width = k.shape
    groups = spec.shape[2]
    rest = rows - BLOCK
    step = pl.program_id(0)
    count = w.shape[1]

    @pl.when(step == 0)
    def _():
        acc[...] = jnp.zeros_like(acc)

    head = ahead[: 4 * HALO, :].astype(F32)
    tail = tails[...].astype(F32)
    end = ends[...].astype(F32)
    for at in range(3):
        put(xe.at[at], HALO, end[at * HALO : (at + 1) * HALO])
        put(xe.at[at], 2 * HALO, head[at * HALO : (at + 1) * HALO])
        put(xe.at[at], 0, jnp.zeros((HALO, width), F32))
    news = [[], [], []]
    for h, lanes in halves(width):
        for at in range(3):
            news[at].append(causal(xe.at[at], h, 2 * HALO, HALO, taps_of(w, at, lanes)))
    qs_new, ks_new, vs_new = (jnp.concatenate(x, axis=1) for x in news)
    gated_new = rounded(ks_new * vs_new)
    ggi_new = head[3 * HALO :] * qs_new
    put(xe.at[0], HALO, gated_new)
    for h, lanes in halves(width):
        total = more[:, lanes]
        for j in range(HALO):
            at = lanes.start % groups
            total = total + taps[j : j + 1, at : at + LANES] * xe[0, h, HALO - j : 2 * HALO - j]
        next_out[:, lanes] = rounded(head[3 * HALO :, lanes] * total)
    put(xk, 0, tail[HALO : 2 * HALO])
    put(xk, HALO, k[...].astype(F32))
    put(xv, 0, tail[2 * HALO :])
    put(xv, HALO, v[...].astype(F32))
    fill = 3 * BLOCK - rows - HALO - BLOCK
    for lanes in blocks(width, groups):
        later = jnp.concatenate(
            [ggi_new[:, lanes], ahead[4 * HALO :, lanes].astype(F32), jnp.zeros((fill, groups), F32)],
            axis=0,
        ).astype(BF16)
        ggi_ext = jnp.concatenate([ggi[:, lanes], later], axis=0)
        own = jnp.concatenate([gated[:, lanes], jnp.zeros((WINDOW - rows, groups), BF16)], axis=0)
        for at in range(2):
            win = to_spectrum(whole[...], ggi_ext[at * BLOCK : at * BLOCK + WINDOW])
            gs = to_spectrum(half[...], own[at * BLOCK : (at + 1) * BLOCK])
            acc[0] += gs[:BLOCK] * win[:BLOCK]
            acc[1] += gs[BLOCK:] * win[BLOCK:]
            acc[2] += gs[:BLOCK] * win[BLOCK:] - gs[BLOCK:] * win[:BLOCK]
            prod = times_conj(win, spec)
            if at == 0:
                gg = from_spectrum(low[...], *prod)
                gk = (gg * vs[:BLOCK, lanes]).astype(BF16)
                gv = (gg * ks[:BLOCK, lanes]).astype(BF16)
                span = slice(0, BLOCK)
            else:
                gg = from_spectrum(low[: rest + HALO, :], *prod)
                zero = jnp.zeros((HALO, groups), F32)
                gk = jnp.concatenate(
                    [gg[:rest] * vs[BLOCK:, lanes], gg[rest:] * vs_new[:, lanes], zero], axis=0
                ).astype(BF16)
                gv = jnp.concatenate(
                    [gg[:rest] * ks[BLOCK:, lanes], gg[rest:] * ks_new[:, lanes], zero], axis=0
                ).astype(BF16)
                span = slice(BLOCK, rows + 2 * HALO)
            gk_out[span, lanes] = gk
            gv_out[span, lanes] = gv
            put(yk, span.start, gk.astype(F32), lanes.start)
            put(yv, span.start, gv.astype(F32), lanes.start)
        for h in range(lanes.start // LANES, lanes.stop // LANES):
            here = slice(h * LANES, (h + 1) * LANES)
            sums_out[:HALO, here] = lag_sums(yk, 0, xk, HALO, h, rows, count)
            sums_out[HALO:, here] = lag_sums(yv, 0, xv, HALO, h, rows, count)
    send_out[...] = sums_out[...].astype(BF16)

    @pl.when(step == pl.num_programs(0) - 1)
    def _():
        first = lax.broadcasted_iota(jnp.int32, (BLOCK, groups), 0) == 0
        real = acc[0] + jnp.where(first, 0.0, acc[1])
        imag = jnp.where(first, acc[1], acc[2])
        mscr[...] = from_spectrum(low[...], real, imag).T
        mine = own_out.shape[0]
        share = groups // mine
        for at in range(share):
            part = mscr[pl.ds(pl.multiple_of(lax.rem(me[0] + at, share) * mine, mine), mine)]
            if at == 0:
                own_out[...] = part
            else:
                more_out[at - 1][...] = part.astype(BF16)


def fourth_kernel(gk, gv, near, far, w, gq_in, gk_out, gv_out, gq_out, yq, yk, yv):
    rows, width = gk_out.shape
    put(yk, 0, gk[...].astype(F32))
    put(yv, 0, gv[...].astype(F32))
    put(yq, 0, near[...])
    put(yq, HALO, far[...])
    put(yq, 2 * HALO, jnp.zeros((HALO, width), F32))
    old = gq_in[...].astype(F32)[:HALO]
    for h, lanes in halves(width):
        for i, ref, out in ((1, yk, gk_out), (2, yv, gv_out)):
            weights = taps_of(w, i, lanes)
            for at, size in pieces(rows):
                out[at : at + size, lanes] = anticausal(ref, h, at, size, weights).astype(BF16)
        fixed = anticausal(yq, h, 0, HALO, taps_of(w, 0, lanes))
        gq_out[:, lanes] = jnp.concatenate([old[:, lanes], fixed], axis=0).astype(BF16)


def fifth_kernel(
    q, tails, following, sums, w, g, inner, behind, spec, half, high, gq_in,
    gq_out, sums_out, send_out,
    xq, yq,
):
    width = q.shape[1]
    put(xq, 0, tails[...].astype(F32)[:HALO])
    put(xq, HALO, q[...].astype(F32))
    put(yq, BLOCK, following[...])
    for lanes in blocks(width, spec.shape[2]):
        edge = from_spectrum(high[...], *times(to_spectrum(half[...], behind[:, lanes]), spec))
        put(yq, 0, rounded(g[:, lanes].astype(F32) * (inner[:, lanes] + edge)), lanes.start)
    for h, lanes in halves(width):
        weights = taps_of(w, 0, lanes)
        for at, size in pieces(BLOCK):
            gq_out[at : at + size, lanes] = anticausal(yq, h, at, size, weights).astype(BF16)
        sums_out[:, lanes] = sums[:, lanes] + lag_sums(yq, 0, xq, HALO, h, BLOCK, w.shape[1])
    send_out[...] = sums_out[...].astype(BF16)


def shift(value, axis, steps):
    count = lax.axis_size(axis)
    initial, last = (max(0, -steps), min(count, count - steps))
    return lax.ppermute(value, axis, [(s, s + steps) for s in range(initial, last)])


def gather_rows(value, axis):
    count, rows = lax.axis_size(axis), value.shape[0]
    me = lax.axis_index(axis)
    result = jnp.zeros((count * rows, value.shape[1]), value.dtype)
    result = lax.dynamic_update_slice(result, value, (me * rows, 0))
    for step in range(1, count):
        other = lax.ppermute(value, axis, [(s, (s + step) % count) for s in range(count)])
        result = lax.dynamic_update_slice(result, other, ((me - step) % count * rows, 0))
    return result


def exchange_sum(own, sends, axis):
    count = lax.axis_size(axis)
    total = own
    for step, part in enumerate(sends, 1):
        total = total + lax.ppermute(
            part, axis, [(s, (s + step) % count) for s in range(count)]
        ).astype(F32)
    return total


def sum_over(value, sent, axis, reverse=False):
    count = lax.axis_size(axis)
    if count & (count - 1):
        return lax.psum(value, axis)
    steps = range(count.bit_length() - 1)
    for bit in reversed(steps) if reverse else steps:
        other = lax.ppermute(sent, axis, [(s, s ^ (1 << bit)) for s in range(count)])
        value = value + other.astype(F32)
        sent = value.astype(BF16)
    return value


def in_hbm(value):
    return pltpu.with_memory_space_constraint(value, pltpu.HBM)


def shards(query, key, value, grad_out, short_filter, medium_filter):
    rows, channels = query.shape
    groups = medium_filter.shape[0] * lax.axis_size("fsdp")
    width = groups
    rest = rows - BLOCK
    taps_short = short_filter.shape[1]
    whole, half, low, high = (jnp.asarray(m) for m in transforms())

    def col(count, at=0, wide=width):
        return pl.BlockSpec((count, wide), lambda i: (at, i))

    def fixed(shape):
        return pl.BlockSpec(shape, lambda i: (0,) * len(shape))

    def filters(wide=width):
        return pl.BlockSpec((3, taps_short, wide), lambda i: (0, 0, i))

    def out(count, dtype):
        return jax.ShapeDtypeStruct((count, channels), dtype)

    def scratch(count, wide=width):
        return pltpu.VMEM((wide // LANES, count, LANES), F32)

    def cost(flops, moved):
        return pl.CostEstimate(flops=int(flops), bytes_accessed=int(moved), transcendentals=0)

    wide = 2 * width
    last = rows // (2 * HALO) - 1
    tails, ahead = pl.pallas_call(
        first_kernel,
        grid=(channels // wide,),
        in_specs=[col(BLOCK + 2 * HALO, 0, wide)] * 2
        + [col(2 * HALO, last, wide)] * 3
        + [col(2 * HALO, 0, wide)] * 2
        + [filters(wide)],
        out_specs=[col(3 * HALO, 0, wide), col(BLOCK + 4 * HALO, 0, wide)],
        out_shape=[out(3 * HALO, BF16), out(BLOCK + 4 * HALO, BF16)],
        scratch_shapes=[scratch(BLOCK + 2 * HALO, wide)],
        name="first",
    )(query, grad_out, query, key, value, key, value, short_filter)
    ends = tails
    tails = in_hbm(shift(tails, "seq", 1))
    ahead = in_hbm(shift(ahead, "seq", -1))
    taps = gather_rows(medium_filter.astype(BF16), "fsdp")

    gated, ggi, ks, vs, inner, behind, spec = pl.pallas_call(
        second_kernel,
        grid=(channels // wide,),
        in_specs=[col(rows, 0, wide)] * 4
        + [col(3 * HALO, 0, wide), filters(wide), fixed(taps.shape), fixed(half.shape), fixed(low.shape)],
        out_specs=[col(rows, 0, wide)] * 4 + [col(BLOCK, 0, wide)] * 2 + [ fixed((3, BLOCK, width))],
        out_shape=[
            out(rows, BF16), out(rows, BF16), out(rows, F32), out(rows, F32),
            out(BLOCK, F32), out(BLOCK, BF16), jax.ShapeDtypeStruct((3, BLOCK, width), F32),
        ],
        scratch_shapes=[scratch(rows + HALO, wide)] * 3 + [pltpu.VMEM((3, BLOCK, width), F32)],
        cost_estimate=cost(4e9, 20e6),
        name="second",
    )(query, key, value, grad_out, tails, short_filter, taps, half, low)
    behind = in_hbm(shift(behind, "seq", 1))

    share = lax.axis_size("fsdp")
    me = lax.axis_index("fsdp").astype(jnp.int32).reshape(1)
    many = channels // wide

    def big(count, at=0):
        return pl.BlockSpec((count, wide), lambda i, *_: (at, i))

    def still(shape):
        return pl.BlockSpec(shape, lambda i, *_: (0,) * len(shape))

    big_filters = pl.BlockSpec((3, taps_short, wide), lambda i, *_: (0, 0, i))
    tap_rows = taps[:, :HALO].astype(F32).T
    corner = BLOCK // rest
    edge_block = rows // (2 * HALO) - 1
    grad_query, nexts, sums_q, more = pl.pallas_call(
        middle_kernel,
        grid=(many,),
        in_specs=[big(rows), big(rest, corner), big(rows), big_filters]
        + [still((3, BLOCK, width)), still(whole.shape), still(high.shape)],
        out_specs=[big(rest, corner), big(2 * HALO), big(HALO), big(HALO)],
        out_shape=[out(rows, BF16), out(2 * HALO, F32), out(HALO, F32), out(HALO, F32)],
        scratch_shapes=[scratch(rest + 2 * HALO, wide)] * 2,
        cost_estimate=cost(2e9, 8e6),
        name="middle",
    )(query, grad_out, gated, short_filter, spec, whole, high)

    mine = (width // share, BLOCK)
    gk, gv, far, sums_kv, sent_kv, own, *sends = pl.pallas_call(
        third_kernel,
        grid_spec=pltpu.PrefetchScalarGridSpec(
            num_scalar_prefetch=1,
            grid=(many,),
            in_specs=[big(rows)] * 2
            + [big(3 * HALO)] * 2
            + [big(BLOCK + 4 * HALO)]
            + [big(rows)] * 4
            + [big(HALO), still(tap_rows.shape), big_filters, still((3, BLOCK, width))]
            + [still(m.shape) for m in (half, whole, low)],
            out_specs=[big(rows + 2 * HALO)] * 2
            + [big(HALO)]
            + [big(2 * HALO)] * 2
            + [still(mine)] * share,
            scratch_shapes=[pltpu.VMEM((3, wide // LANES, 3 * HALO, LANES), F32)]
            + [scratch(rows + 2 * HALO, wide)] * 4
            + [pltpu.VMEM((3, BLOCK, width), F32), pltpu.VMEM((width, BLOCK), F32)],
        ),
        out_shape=[out(rows + 2 * HALO, BF16)] * 2
        + [out(HALO, F32), out(2 * HALO, F32), out(2 * HALO, BF16)]
        + [jax.ShapeDtypeStruct(mine, F32)]
        + [jax.ShapeDtypeStruct(mine, BF16)] * (share - 1),
        cost_estimate=cost(8e9, 20e6),
        name="third",
    )(me, key, value, tails, ends, ahead, gated, ggi, ks, vs, more, tap_rows,
      short_filter, spec, half, whole, low)
    medium = exchange_sum(own, sends, "fsdp")

    grad_key, grad_value, grad_query = pl.pallas_call(
        fourth_kernel,
        grid=(many,),
        in_specs=[big(rows + 2 * HALO)] * 2
        + [big(HALO, 1), big(HALO), big_filters, big(2 * HALO, edge_block)],
        out_specs=[big(rows), big(rows), big(2 * HALO, edge_block)],
        out_shape=[out(rows, BF16)] * 3,
        scratch_shapes=[scratch(3 * HALO, wide)] + [scratch(rows + 2 * HALO, wide)] * 2,
        input_output_aliases={5: 2},
        cost_estimate=cost(4e9, 10e6),
        name="fourth",
    )(gk, gv, nexts, far, short_filter, grad_query)

    grad_query, sums_q, sent_q = pl.pallas_call(
        fifth_kernel,
        grid=(many,),
        in_specs=[big(BLOCK), big(3 * HALO), big(HALO), big(HALO), big_filters]
        + [big(BLOCK)] * 3
        + [still((3, BLOCK, width)), still(half.shape), still(high.shape)]
        + [pl.BlockSpec(memory_space=pl.ANY)],
        out_specs=[big(BLOCK), big(HALO), big(HALO)],
        out_shape=[out(rows, BF16), out(HALO, F32), out(HALO, BF16)],
        scratch_shapes=[scratch(BLOCK + HALO, wide)] * 2,
        input_output_aliases={11: 0},
        cost_estimate=cost(2e9, 8e6),
        name="fifth",
    )(query, tails, nexts, sums_q, short_filter, grad_out, inner, behind, spec, half, high,
      grad_query)

    per = channels // BLOCK
    count = medium.shape[0] // per
    packed = jnp.concatenate([medium[i * count : (i + 1) * count] for i in range(per)], axis=1)
    early = jnp.concatenate([sums_kv, packed], axis=0)
    sent = jnp.concatenate([sent_kv, packed.astype(BF16)], axis=0)
    early = sum_over(early, sent, "seq", reverse=True)
    late = sum_over(sums_q, sent_q, "seq")
    packed = early[2 * HALO :]
    grad_medium = jnp.concatenate([packed[:, i * BLOCK : (i + 1) * BLOCK] for i in range(per)], axis=0)
    grad_short = jnp.stack([late[:taps_short], early[:taps_short], early[HALO : HALO + taps_short]])
    return grad_query, grad_key, grad_value, grad_short, grad_medium


def solution(mesh):
    in_specs = (
        P("seq", "fsdp"),
        P("seq", "fsdp"),
        P("seq", "fsdp"),
        P("seq", "fsdp"),
        P(None, None, "fsdp"),
        P("fsdp", None),
    )
    out_specs = (
        P("seq", "fsdp"),
        P("seq", "fsdp"),
        P("seq", "fsdp"),
        P(None, None, "fsdp"),
        P("fsdp", None),
    )
    return jax.shard_map(shards, mesh=mesh, in_specs=in_specs, out_specs=out_specs, check_vma=False)
```

```python
import numpy as np
import jax
import jax.numpy as jnp
from jax import lax
from jax.experimental import pallas as pl
from jax.experimental.pallas import tpu as pltpu
from jax.sharding import PartitionSpec as P


HALO = 8
BLOCK = 128
WINDOW = 2 * BLOCK
F32 = jnp.float32
BF16 = jnp.bfloat16


def split_terms(matrix):
    high = matrix.astype(BF16)
    low = (matrix - high.astype(np.float32)).astype(BF16)
    return np.asarray(high), np.asarray(low)


def transforms():
    time = np.arange(WINDOW)
    freq = np.arange(BLOCK)
    angle = 2 * np.pi * ((freq[:, None] * time[None, :]) % WINDOW) / WINDOW
    cosine, sine = np.cos(angle), np.sin(angle)
    nyquist = np.where(time % 2 == 0, 1.0, -1.0)
    forward = np.concatenate([cosine, -sine]).astype(np.float64)
    forward[BLOCK] = nyquist
    scale = np.full(WINDOW, 2.0 / WINDOW)
    scale[0] = scale[BLOCK] = 1.0 / WINDOW
    inverse = forward.T * scale[None, :]
    f_high, f_low = split_terms(forward.astype(np.float32))
    i_high, i_low = split_terms(inverse.astype(np.float32))
    whole = np.concatenate([f_high, f_low], axis=1)
    half = np.concatenate([f_high[:, :BLOCK], f_low[:, :BLOCK]], axis=1)
    back = np.concatenate([i_high, i_low], axis=1)
    return whole, half, back[:BLOCK], back[BLOCK:]


def dot(left, right):
    return jnp.dot(left, right, preferred_element_type=F32)


def to_spectrum(matrix, rows):
    return dot(matrix, jnp.concatenate([rows, rows], axis=0))


def from_spectrum(matrix, real, imag):
    whole = jnp.concatenate([real, imag], axis=0).astype(BF16)
    return to_spectrum(matrix, whole)


def times(spec, taps):
    xr, xi = spec[:BLOCK], spec[BLOCK:]
    return xr * taps[0] - xi * taps[1], xr * taps[1] + xi * taps[2]


def times_conj(spec, taps):
    xr, xi = spec[:BLOCK], spec[BLOCK:]
    return xr * taps[0] + xi * taps[1], xi * taps[2] - xr * taps[1]


def blocks(wide, width):
    return [slice(at, at + width) for at in range(0, wide, width)]


def rounded(value):
    return value.astype(BF16).astype(F32)


LANES = 128
ROOM = 40 * 1024 * 1024
CHUNK = 64


def halves(width):
    return [(at // LANES, slice(at, at + LANES)) for at in range(0, width, LANES)]


def pieces(count):
    return [(at, min(CHUNK, count - at)) for at in range(0, count, CHUNK)]


def put(ref, at, value, lane=0):
    for h, lanes in halves(value.shape[1]):
        ref[h + lane // LANES, at : at + value.shape[0]] = value[:, lanes]


def causal(ref, h, at, count, weights):
    total = None
    for j, weight in enumerate(weights):
        term = weight * ref[h, at - j : at - j + count]
        total = term if total is None else total + term
    return total


def anticausal(ref, h, at, count, weights):
    total = None
    for j, weight in enumerate(weights):
        term = weight * ref[h, at + j : at + j + count]
        total = term if total is None else total + term
    return total


def taps_of(w, index, lanes):
    return [w[index, j : j + 1, lanes] for j in range(w.shape[1])]


def lag_sums(grad, g_at, x, x_at, h, count, taps):
    totals = [None] * taps
    for at, size in pieces(count):
        mine = grad[h, g_at + at : g_at + at + size]
        for j in range(taps):
            prod = mine * x[h, x_at + at - j : x_at + at - j + size]
            part = jnp.sum(prod.reshape(size // 8, 8, LANES), axis=0)
            totals[j] = part if totals[j] is None else totals[j] + part
    rows = [jnp.sum(t, axis=0, keepdims=True) for t in totals]
    return jnp.concatenate(rows + [jnp.zeros_like(rows[0])], axis=0)


def first_kernel(q, g, q_tail, k_tail, v_tail, k_head, v_head, w, tails, ahead, xq):
    tails[...] = jnp.concatenate(
        [x[...].astype(F32)[HALO:] for x in (q_tail, k_tail, v_tail)], axis=0
    ).astype(BF16)
    put(xq, 0, q[...].astype(F32))
    grad = g[...].astype(F32)
    heads = [x[: 2 * HALO, :].astype(F32)[:HALO] for x in (q, k_head, v_head, g)]
    ahead[: 4 * HALO] = jnp.concatenate(heads, axis=0).astype(BF16)
    for h, lanes in halves(q.shape[1]):
        weights = taps_of(w, 0, lanes)
        for at, size in pieces(BLOCK):
            qs = causal(xq, h, HALO + at, size, weights)
            ahead[4 * HALO + at : 4 * HALO + at + size, lanes] = (
                grad[HALO + at : HALO + at + size, lanes] * qs
            ).astype(BF16)


def second_kernel(
    q, k, v, g, tails, w, taps, half, low,
    gated_out, ggi_out, ks_out, vs_out, inner_out, behind_out, spec_out, rows_out,
    xq, xk, xv, tap_spec,
):
    rows, width = q.shape

    @pl.when(pl.program_id(0) == 0)
    def _():
        both = jnp.concatenate([taps[...], taps[...]], axis=1)
        spec = lax.dot_general(half[...], both, (((1,), (1,)), ((), ())), preferred_element_type=F32)
        real, imag = spec[:BLOCK], spec[BLOCK:]
        first = lax.broadcasted_iota(jnp.int32, real.shape, 0) == 0
        tap_spec[0] = real
        tap_spec[1] = jnp.where(first, 0.0, imag)
        tap_spec[2] = jnp.where(first, imag, real)
        spec_out[...] = tap_spec[...]
        rows_out[...] = taps[...].astype(F32).T[:HALO]

    tail = tails[...].astype(F32)
    for at, (ref, x) in enumerate(((xq, q), (xk, k), (xv, v))):
        put(ref, 0, tail[at * HALO : (at + 1) * HALO])
        put(ref, HALO, x[...].astype(F32))
    for h, lanes in halves(width):
        wq, wk, wv = (taps_of(w, i, lanes) for i in range(3))
        for at, size in pieces(rows):
            span = slice(at, at + size)
            ks = causal(xk, h, HALO + at, size, wk)
            vs = causal(xv, h, HALO + at, size, wv)
            ks_out[span, lanes] = ks
            vs_out[span, lanes] = vs
            gated_out[span, lanes] = (ks * vs).astype(BF16)
            qs = causal(xq, h, HALO + at, size, wq)
            ggi_out[span, lanes] = (g[span, lanes].astype(F32) * qs).astype(BF16)
    behind_out[...] = gated_out[rows - BLOCK :, :]
    for lanes in blocks(width, taps.shape[0]):
        first = to_spectrum(half[...], gated_out[:BLOCK, lanes])
        inner_out[:, lanes] = from_spectrum(low[...], *times(first, tap_spec))


def middle_kernel(
    q, g, gated, w, spec, whole, high,
    gq_out, next_out, sums_out, more_out,
    xq, yq,
):
    rows, width = gated.shape
    rest = rows - BLOCK
    for lanes in blocks(width, spec.shape[2]):
        wide = lanes.stop - lanes.start
        window = jnp.concatenate(
            [gated[:, lanes], jnp.zeros((WINDOW - rows, wide), BF16)], axis=0
        )
        prod = times(to_spectrum(whole[...], window), spec)
        sig = from_spectrum(high[: rest + HALO, :], *prod)
        put(yq, 0, rounded(g[:, lanes].astype(F32) * sig[:rest]), lanes.start)
        more_out[:, lanes] = sig[rest:]
    put(xq, 0, q[BLOCK - 2 * HALO :, :].astype(F32))
    for h, lanes in halves(width):
        next_out[:HALO, lanes] = yq[h, :HALO]
        next_out[HALO:, lanes] = yq[h, rest - HALO : rest]
        gq_out[:, lanes] = anticausal(yq, h, 0, rest, taps_of(w, 0, lanes)).astype(BF16)
        sums_out[:, lanes] = lag_sums(yq, 0, xq, 2 * HALO, h, rest, w.shape[1])


def third_kernel(
    me, k, v, tails, ends, ahead, gated, ggi, ks, vs, more, taps, w, spec, half, whole, low,
    gk_out, gv_out, next_out, sums_out, send_out, own_out, *rest_refs,
):
    *more_out, xe, xk, xv, yk, yv, acc, mscr = rest_refs
    rows, width = k.shape
    groups = spec.shape[2]
    rest = rows - BLOCK
    step = pl.program_id(0)
    count = w.shape[1]

    @pl.when(step == 0)
    def _():
        acc[...] = jnp.zeros_like(acc)

    head = ahead[: 4 * HALO, :].astype(F32)
    tail = tails[...].astype(F32)
    end = ends[...].astype(F32)
    for at in range(3):
        put(xe.at[at], HALO, end[at * HALO : (at + 1) * HALO])
        put(xe.at[at], 2 * HALO, head[at * HALO : (at + 1) * HALO])
        put(xe.at[at], 0, jnp.zeros((HALO, width), F32))
    news = [[], [], []]
    for h, lanes in halves(width):
        for at in range(3):
            news[at].append(causal(xe.at[at], h, 2 * HALO, HALO, taps_of(w, at, lanes)))
    qs_new, ks_new, vs_new = (jnp.concatenate(x, axis=1) for x in news)
    gated_new = rounded(ks_new * vs_new)
    ggi_new = head[3 * HALO :] * qs_new
    put(xe.at[0], HALO, gated_new)
    for h, lanes in halves(width):
        total = more[:, lanes]
        for j in range(HALO):
            at = lanes.start % groups
            total = total + taps[j : j + 1, at : at + LANES] * xe[0, h, HALO - j : 2 * HALO - j]
        next_out[:, lanes] = rounded(head[3 * HALO :, lanes] * total)
    put(xk, 0, tail[HALO : 2 * HALO])
    put(xk, HALO, k[...].astype(F32))
    put(xv, 0, tail[2 * HALO :])
    put(xv, HALO, v[...].astype(F32))
    fill = 3 * BLOCK - rows - HALO - BLOCK
    for lanes in blocks(width, groups):
        later = jnp.concatenate(
            [ggi_new[:, lanes], ahead[4 * HALO :, lanes].astype(F32), jnp.zeros((fill, groups), F32)],
            axis=0,
        ).astype(BF16)
        ggi_ext = jnp.concatenate([ggi[:, lanes], later], axis=0)
        own = jnp.concatenate([gated[:, lanes], jnp.zeros((WINDOW - rows, groups), BF16)], axis=0)
        for at in range(2):
            win = to_spectrum(whole[...], ggi_ext[at * BLOCK : at * BLOCK + WINDOW])
            gs = to_spectrum(half[...], own[at * BLOCK : (at + 1) * BLOCK])
            acc[0] += gs[:BLOCK] * win[:BLOCK]
            acc[1] += gs[BLOCK:] * win[BLOCK:]
            acc[2] += gs[:BLOCK] * win[BLOCK:] - gs[BLOCK:] * win[:BLOCK]
            prod = times_conj(win, spec)
            if at == 0:
                gg = from_spectrum(low[...], *prod)
                gk = (gg * vs[:BLOCK, lanes]).astype(BF16)
                gv = (gg * ks[:BLOCK, lanes]).astype(BF16)
                span = slice(0, BLOCK)
            else:
                gg = from_spectrum(low[: rest + HALO, :], *prod)
                zero = jnp.zeros((HALO, groups), F32)
                gk = jnp.concatenate(
                    [gg[:rest] * vs[BLOCK:, lanes], gg[rest:] * vs_new[:, lanes], zero], axis=0
                ).astype(BF16)
                gv = jnp.concatenate(
                    [gg[:rest] * ks[BLOCK:, lanes], gg[rest:] * ks_new[:, lanes], zero], axis=0
                ).astype(BF16)
                span = slice(BLOCK, rows + 2 * HALO)
            gk_out[span, lanes] = gk
            gv_out[span, lanes] = gv
            put(yk, span.start, gk.astype(F32), lanes.start)
            put(yv, span.start, gv.astype(F32), lanes.start)
        for h in range(lanes.start // LANES, lanes.stop // LANES):
            here = slice(h * LANES, (h + 1) * LANES)
            sums_out[:HALO, here] = lag_sums(yk, 0, xk, HALO, h, rows, count)
            sums_out[HALO:, here] = lag_sums(yv, 0, xv, HALO, h, rows, count)
    send_out[...] = sums_out[...].astype(BF16)

    @pl.when(step == pl.num_programs(0) - 1)
    def _():
        first = lax.broadcasted_iota(jnp.int32, (BLOCK, groups), 0) == 0
        real = acc[0] + jnp.where(first, 0.0, acc[1])
        imag = jnp.where(first, acc[1], acc[2])
        mscr[...] = from_spectrum(low[...], real, imag).T
        mine = own_out.shape[0]
        share = groups // mine
        for at in range(share):
            part = mscr[pl.ds(pl.multiple_of(lax.rem(me[0] + at, share) * mine, mine), mine)]
            if at == 0:
                own_out[...] = part
            else:
                more_out[at - 1][...] = part.astype(BF16)


def fourth_kernel(gk, gv, near, far, w, gq_in, gk_out, gv_out, gq_out, yq, yk, yv):
    rows, width = gk_out.shape
    put(yk, 0, gk[...].astype(F32))
    put(yv, 0, gv[...].astype(F32))
    put(yq, 0, near[...])
    put(yq, HALO, far[...])
    put(yq, 2 * HALO, jnp.zeros((HALO, width), F32))
    old = gq_in[...].astype(F32)[:HALO]
    for h, lanes in halves(width):
        for i, ref, out in ((1, yk, gk_out), (2, yv, gv_out)):
            weights = taps_of(w, i, lanes)
            for at, size in pieces(rows):
                out[at : at + size, lanes] = anticausal(ref, h, at, size, weights).astype(BF16)
        fixed = anticausal(yq, h, 0, HALO, taps_of(w, 0, lanes))
        gq_out[:, lanes] = jnp.concatenate([old[:, lanes], fixed], axis=0).astype(BF16)


def fifth_kernel(
    q, tails, following, sums, w, g, inner, behind, spec, half, high, gq_in, own, *refs,
):
    *parts, gq_out, sums_out, send_out, xq, yq = refs
    width = q.shape[1]
    total = own[...]
    for part in parts:
        total = total + part[...].astype(F32)
    count = total.shape[0] // (width // LANES)
    for h, lanes in halves(width):
        sums_out[HALO:, lanes] = total[h * count : (h + 1) * count]
    put(xq, 0, tails[...].astype(F32)[:HALO])
    put(xq, HALO, q[...].astype(F32))
    put(yq, BLOCK, following[...])
    for lanes in blocks(width, spec.shape[2]):
        edge = from_spectrum(high[...], *times(to_spectrum(half[...], behind[:, lanes]), spec))
        put(yq, 0, rounded(g[:, lanes].astype(F32) * (inner[:, lanes] + edge)), lanes.start)
    for h, lanes in halves(width):
        weights = taps_of(w, 0, lanes)
        for at, size in pieces(BLOCK):
            gq_out[at : at + size, lanes] = anticausal(yq, h, at, size, weights).astype(BF16)
        sums_out[:HALO, lanes] = sums[:, lanes] + lag_sums(yq, 0, xq, HALO, h, BLOCK, w.shape[1])
    send_out[...] = sums_out[...].astype(BF16)


def shift(value, axis, steps):
    count = lax.axis_size(axis)
    initial, last = (max(0, -steps), min(count, count - steps))
    return lax.ppermute(value, axis, [(s, s + steps) for s in range(initial, last)])


def gather_rows(value, axis):
    count, rows = lax.axis_size(axis), value.shape[0]
    me = lax.axis_index(axis)
    result = jnp.zeros((count * rows, value.shape[1]), value.dtype)
    result = lax.dynamic_update_slice(result, value, (me * rows, 0))
    for step in range(1, count):
        other = lax.ppermute(value, axis, [(s, (s + step) % count) for s in range(count)])
        result = lax.dynamic_update_slice(result, other, ((me - step) % count * rows, 0))
    return result


def exchanged(sends, axis):
    count = lax.axis_size(axis)
    return [
        lax.ppermute(part, axis, [(s, (s + step) % count) for s in range(count)])
        for step, part in enumerate(sends, 1)
    ]


def sum_over(value, sent, axis, reverse=False):
    count = lax.axis_size(axis)
    if count & (count - 1):
        return lax.psum(value, axis)
    steps = range(count.bit_length() - 1)
    for bit in reversed(steps) if reverse else steps:
        other = lax.ppermute(sent, axis, [(s, s ^ (1 << bit)) for s in range(count)])
        value = value + other.astype(F32)
        sent = value.astype(BF16)
    return value


def in_hbm(value):
    return pltpu.with_memory_space_constraint(value, pltpu.HBM)


def shards(query, key, value, grad_out, short_filter, medium_filter):
    rows, channels = query.shape
    groups = medium_filter.shape[0] * lax.axis_size("fsdp")
    width = groups
    rest = rows - BLOCK
    taps_short = short_filter.shape[1]
    whole, half, low, high = (jnp.asarray(m) for m in transforms())

    def col(count, at=0, wide=width):
        return pl.BlockSpec((count, wide), lambda i: (at, i))

    def fixed(shape):
        return pl.BlockSpec(shape, lambda i: (0,) * len(shape))

    def filters(wide=width):
        return pl.BlockSpec((3, taps_short, wide), lambda i: (0, 0, i))

    def out(count, dtype):
        return jax.ShapeDtypeStruct((count, channels), dtype)

    def scratch(count, wide=width):
        return pltpu.VMEM((wide // LANES, count, LANES), F32)

    def cost(flops, moved):
        return pl.CostEstimate(flops=int(flops), bytes_accessed=int(moved), transcendentals=0)

    query, key, value, grad_out, short_filter = (
        in_hbm(x) for x in (query, key, value, grad_out, short_filter)
    )
    whole, half, low, high = (in_hbm(x) for x in (whole, half, low, high))
    room = pltpu.CompilerParams(vmem_limit_bytes=ROOM)
    wide = min(4 * width, channels)
    pair = min(2 * width, channels)
    last = rows // (2 * HALO) - 1
    tails, ahead = pl.pallas_call(
        first_kernel,
        grid=(channels // wide,),
        in_specs=[col(BLOCK + 2 * HALO, 0, wide)] * 2
        + [col(2 * HALO, last, wide)] * 3
        + [col(2 * HALO, 0, wide)] * 2
        + [filters(wide)],
        out_specs=[col(3 * HALO, 0, wide), col(BLOCK + 4 * HALO, 0, wide)],
        out_shape=[out(3 * HALO, BF16), out(BLOCK + 4 * HALO, BF16)],
        scratch_shapes=[scratch(BLOCK + 2 * HALO, wide)],
        name="first",
        compiler_params=room,
    )(query, grad_out, query, key, value, key, value, short_filter)
    ends = tails
    tails = shift(tails, "seq", 1)
    ahead = shift(ahead, "seq", -1)
    taps = gather_rows(medium_filter.astype(BF16), "fsdp")

    gated, ggi, ks, vs, inner, behind, spec, tap_rows = pl.pallas_call(
        second_kernel,
        grid=(channels // wide,),
        in_specs=[col(rows, 0, wide)] * 4
        + [col(3 * HALO, 0, wide), filters(wide), fixed(taps.shape), fixed(half.shape), fixed(low.shape)],
        out_specs=[col(rows, 0, wide)] * 4 + [col(BLOCK, 0, wide)] * 2 + [fixed((3, BLOCK, width)), fixed((HALO, width))],
        out_shape=[
            out(rows, BF16), out(rows, BF16), out(rows, F32), out(rows, F32),
            out(BLOCK, F32), out(BLOCK, BF16), jax.ShapeDtypeStruct((3, BLOCK, width), F32),
            jax.ShapeDtypeStruct((HALO, width), F32),
        ],
        scratch_shapes=[scratch(rows + HALO, wide)] * 3 + [pltpu.VMEM((3, BLOCK, width), F32)],
        cost_estimate=cost(4e9, 20e6),
        name="second",
        compiler_params=room,
    )(query, key, value, grad_out, tails, short_filter, taps, half, low)
    behind = shift(behind, "seq", 1)

    share = lax.axis_size("fsdp")
    me = lax.axis_index("fsdp").astype(jnp.int32).reshape(1)
    many = channels // wide

    def big(count, at=0):
        return pl.BlockSpec((count, wide), lambda i, *_: (at, i))

    def two(count, at=0):
        return pl.BlockSpec((count, pair), lambda i, *_: (at, i))

    def still(shape):
        return pl.BlockSpec(shape, lambda i, *_: (0,) * len(shape))

    two_filters = pl.BlockSpec((3, taps_short, pair), lambda i, *_: (0, 0, i))
    big_filters = pl.BlockSpec((3, taps_short, wide), lambda i, *_: (0, 0, i))
    corner = BLOCK // rest
    edge_block = rows // (2 * HALO) - 1
    grad_query, nexts, sums_q, more = pl.pallas_call(
        middle_kernel,
        grid=(many,),
        in_specs=[big(rows), big(rest, corner), big(rows), big_filters]
        + [still((3, BLOCK, width)), still(whole.shape), still(high.shape)],
        out_specs=[big(rest, corner), big(2 * HALO), big(HALO), big(HALO)],
        out_shape=[out(rows, BF16), out(2 * HALO, F32), out(HALO, F32), out(HALO, F32)],
        scratch_shapes=[scratch(rest + 2 * HALO, wide)] * 2,
        cost_estimate=cost(2e9, 8e6),
        name="middle",
        compiler_params=room,
    )(query, grad_out, gated, short_filter, spec, whole, high)

    mine = (width // share, BLOCK)
    gk, gv, far, sums_kv, sent_kv, own, *sends = pl.pallas_call(
        third_kernel,
        grid_spec=pltpu.PrefetchScalarGridSpec(
            num_scalar_prefetch=1,
            grid=(channels // pair,),
            in_specs=[two(rows)] * 2
            + [two(3 * HALO)] * 2
            + [two(BLOCK + 4 * HALO)]
            + [two(rows)] * 4
            + [two(HALO), still(tap_rows.shape), two_filters, still((3, BLOCK, width))]
            + [still(m.shape) for m in (half, whole, low)],
            out_specs=[two(rows + 2 * HALO)] * 2
            + [two(HALO)]
            + [two(2 * HALO)] * 2
            + [still(mine)] * share,
            scratch_shapes=[pltpu.VMEM((3, pair // LANES, 3 * HALO, LANES), F32)]
            + [scratch(rows + 2 * HALO, pair)] * 4
            + [pltpu.VMEM((3, BLOCK, width), F32), pltpu.VMEM((width, BLOCK), F32)],
        ),
        out_shape=[out(rows + 2 * HALO, BF16)] * 2
        + [out(HALO, F32), out(2 * HALO, F32), out(2 * HALO, BF16)]
        + [jax.ShapeDtypeStruct(mine, F32)]
        + [jax.ShapeDtypeStruct(mine, BF16)] * (share - 1),
        cost_estimate=cost(8e9, 20e6),
        name="third",
        compiler_params=room,
    )(me, key, value, tails, ends, ahead, gated, ggi, ks, vs, more, tap_rows,
      short_filter, spec, half, whole, low)
    parts = exchanged(sends, "fsdp")

    grad_key, grad_value, grad_query = pl.pallas_call(
        fourth_kernel,
        grid=(many,),
        in_specs=[big(rows + 2 * HALO)] * 2
        + [big(HALO, 1), big(HALO), big_filters, big(2 * HALO, edge_block)],
        out_specs=[big(rows), big(rows), big(2 * HALO, edge_block)],
        out_shape=[out(rows, BF16)] * 3,
        scratch_shapes=[scratch(3 * HALO, wide)] + [scratch(rows + 2 * HALO, wide)] * 2,
        input_output_aliases={5: 2},
        cost_estimate=cost(4e9, 10e6),
        name="fourth",
        compiler_params=room,
    )(gk, gv, nexts, far, short_filter, grad_query)

    extra = mine[0] * BLOCK // channels
    grad_query, sums_q, sent_q = pl.pallas_call(
        fifth_kernel,
        grid=(many,),
        in_specs=[big(BLOCK), big(3 * HALO), big(HALO), big(HALO), big_filters]
        + [big(BLOCK)] * 3
        + [still((3, BLOCK, width)), still(half.shape), still(high.shape)]
        + [pl.BlockSpec(memory_space=pl.ANY)]
        + [pl.BlockSpec((mine[0] * wide // channels, BLOCK), lambda i: (i, 0))] * share,
        out_specs=[big(BLOCK), big(HALO + extra), big(HALO + extra)],
        out_shape=[out(rows, BF16), out(HALO + extra, F32), out(HALO + extra, BF16)],
        scratch_shapes=[scratch(BLOCK + HALO, wide)] * 2,
        input_output_aliases={11: 0},
        cost_estimate=cost(2e9, 8e6),
        name="fifth",
        compiler_params=room,
    )(query, tails, nexts, sums_q, short_filter, grad_out, inner, behind, spec, half, high,
      grad_query, own, *parts)

    early = sum_over(sums_kv, sent_kv, "seq", reverse=True)
    late = sum_over(sums_q, sent_q, "seq")
    packed = late[HALO:]
    grad_medium = jnp.concatenate(
        [packed[:, at : at + BLOCK] for at in range(0, channels, BLOCK)], axis=0
    )
    grad_short = jnp.stack([late[:taps_short], early[:taps_short], early[HALO : HALO + taps_short]])
    return grad_query, grad_key, grad_value, grad_short, grad_medium


def solution(mesh):
    in_specs = (
        P("seq", "fsdp"),
        P("seq", "fsdp"),
        P("seq", "fsdp"),
        P("seq", "fsdp"),
        P(None, None, "fsdp"),
        P("fsdp", None),
    )
    out_specs = (
        P("seq", "fsdp"),
        P("seq", "fsdp"),
        P("seq", "fsdp"),
        P(None, None, "fsdp"),
        P("fsdp", None),
    )
    return jax.shard_map(shards, mesh=mesh, in_specs=in_specs, out_specs=out_specs, check_vma=False)
```

```python
import numpy as np
import jax
import jax.numpy as jnp
from jax import lax
from jax.experimental import pallas as pl
from jax.experimental.pallas import tpu as pltpu
from jax.sharding import PartitionSpec as P


HALO = 8
BLOCK = 128
WINDOW = 2 * BLOCK
F32 = jnp.float32
BF16 = jnp.bfloat16


def split_terms(matrix):
    high = matrix.astype(BF16)
    low = (matrix - high.astype(np.float32)).astype(BF16)
    return np.asarray(high), np.asarray(low)


def transforms():
    time = np.arange(WINDOW)
    freq = np.arange(BLOCK)
    angle = 2 * np.pi * ((freq[:, None] * time[None, :]) % WINDOW) / WINDOW
    cosine, sine = np.cos(angle), np.sin(angle)
    nyquist = np.where(time % 2 == 0, 1.0, -1.0)
    forward = np.concatenate([cosine, -sine]).astype(np.float64)
    forward[BLOCK] = nyquist
    scale = np.full(WINDOW, 2.0 / WINDOW)
    scale[0] = scale[BLOCK] = 1.0 / WINDOW
    inverse = forward.T * scale[None, :]
    f_high, f_low = split_terms(forward.astype(np.float32))
    i_high, i_low = split_terms(inverse.astype(np.float32))
    whole = np.concatenate([f_high, f_low], axis=1)
    half = np.concatenate([f_high[:, :BLOCK], f_low[:, :BLOCK]], axis=1)
    back = np.concatenate([i_high, i_low], axis=1)
    return whole, half, back[:BLOCK], back[BLOCK:]


def dot(left, right):
    return jnp.dot(left, right, preferred_element_type=F32)


def to_spectrum(matrix, rows):
    return dot(matrix, jnp.concatenate([rows, rows], axis=0))


def from_spectrum(matrix, real, imag):
    whole = jnp.concatenate([real, imag], axis=0).astype(BF16)
    return to_spectrum(matrix, whole)


def times(spec, taps):
    xr, xi = spec[:BLOCK], spec[BLOCK:]
    return xr * taps[0] - xi * taps[1], xr * taps[1] + xi * taps[2]


def times_conj(spec, taps):
    xr, xi = spec[:BLOCK], spec[BLOCK:]
    return xr * taps[0] + xi * taps[1], xi * taps[2] - xr * taps[1]


def blocks(wide, width):
    return [slice(at, at + width) for at in range(0, wide, width)]


def rounded(value):
    return value.astype(BF16).astype(F32)


LANES = 128
ROOM = 40 * 1024 * 1024
CHUNK = 64


def halves(width):
    return [(at // LANES, slice(at, at + LANES)) for at in range(0, width, LANES)]


def pieces(count):
    return [(at, min(CHUNK, count - at)) for at in range(0, count, CHUNK)]


def put(ref, at, value, lane=0):
    for h, lanes in halves(value.shape[1]):
        ref[h + lane // LANES, at : at + value.shape[0]] = value[:, lanes]


def causal(ref, h, at, count, weights):
    total = None
    for j, weight in enumerate(weights):
        term = weight * ref[h, at - j : at - j + count]
        total = term if total is None else total + term
    return total


def anticausal(ref, h, at, count, weights):
    total = None
    for j, weight in enumerate(weights):
        term = weight * ref[h, at + j : at + j + count]
        total = term if total is None else total + term
    return total


def taps_of(w, index, lanes):
    return [w[index, j : j + 1, lanes] for j in range(w.shape[1])]


def lag_sums(grad, g_at, x, x_at, h, count, taps):
    totals = [None] * taps
    for at, size in pieces(count):
        mine = grad[h, g_at + at : g_at + at + size]
        for j in range(taps):
            prod = mine * x[h, x_at + at - j : x_at + at - j + size]
            part = jnp.sum(prod.reshape(size // 8, 8, LANES), axis=0)
            totals[j] = part if totals[j] is None else totals[j] + part
    rows = [jnp.sum(t, axis=0, keepdims=True) for t in totals]
    return jnp.concatenate(rows + [jnp.zeros_like(rows[0])], axis=0)


def first_kernel(q, g, q_tail, k_tail, v_tail, k_head, v_head, w, tails, ahead, xq):
    tails[...] = jnp.concatenate(
        [x[...].astype(F32)[HALO:] for x in (q_tail, k_tail, v_tail)], axis=0
    ).astype(BF16)
    put(xq, 0, q[...].astype(F32))
    grad = g[...].astype(F32)
    heads = [x[: 2 * HALO, :].astype(F32)[:HALO] for x in (q, k_head, v_head, g)]
    ahead[: 4 * HALO] = jnp.concatenate(heads, axis=0).astype(BF16)
    for h, lanes in halves(q.shape[1]):
        weights = taps_of(w, 0, lanes)
        for at, size in pieces(BLOCK):
            qs = causal(xq, h, HALO + at, size, weights)
            ahead[4 * HALO + at : 4 * HALO + at + size, lanes] = (
                grad[HALO + at : HALO + at + size, lanes] * qs
            ).astype(BF16)


def second_kernel(
    q, k, v, g, tails, w,
    gated_out, ggi_out, ks_out, vs_out, behind_out,
    xq, xk, xv,
):
    rows, width = q.shape
    tail = tails[...].astype(F32)
    for at, (ref, x) in enumerate(((xq, q), (xk, k), (xv, v))):
        put(ref, 0, tail[at * HALO : (at + 1) * HALO])
        put(ref, HALO, x[...].astype(F32))
    for h, lanes in halves(width):
        wq, wk, wv = (taps_of(w, i, lanes) for i in range(3))
        for at, size in pieces(rows):
            span = slice(at, at + size)
            ks = causal(xk, h, HALO + at, size, wk)
            vs = causal(xv, h, HALO + at, size, wv)
            ks_out[span, lanes] = ks
            vs_out[span, lanes] = vs
            gated_out[span, lanes] = (ks * vs).astype(BF16)
            qs = causal(xq, h, HALO + at, size, wq)
            ggi_out[span, lanes] = (g[span, lanes].astype(F32) * qs).astype(BF16)
    behind_out[...] = gated_out[rows - BLOCK :, :]


def middle_kernel(me, q, g, gated, w, half, whole, high, own_taps, *refs):
    *more_taps, gq_out, next_out, sums_out, more_out, spec_out, rows_out, xq, yq, spec, taps = refs
    rows, width = gated.shape
    rest = rows - BLOCK
    groups = taps.shape[0]

    @pl.when(pl.program_id(0) == 0)
    def _():
        mine = own_taps.shape[0]
        share = groups // mine
        for at, part in enumerate([own_taps] + more_taps):
            place = lax.rem(me[0] + share - at, share) * mine
            taps[pl.ds(pl.multiple_of(place, mine), mine)] = part[...].astype(BF16).astype(F32)
        whole_taps = taps[...].astype(BF16)
        both = jnp.concatenate([whole_taps, whole_taps], axis=1)
        whole_spec = lax.dot_general(
            half[...], both, (((1,), (1,)), ((), ())), preferred_element_type=F32
        )
        real, imag = whole_spec[:BLOCK], whole_spec[BLOCK:]
        first = lax.broadcasted_iota(jnp.int32, real.shape, 0) == 0
        spec[0] = real
        spec[1] = jnp.where(first, 0.0, imag)
        spec[2] = jnp.where(first, imag, real)
        spec_out[...] = spec[...]
        rows_out[...] = taps[...].T[:HALO]

    for lanes in blocks(width, groups):
        pad = jnp.zeros((WINDOW - rows, groups), BF16)
        window = jnp.concatenate([gated[:, lanes], pad], axis=0)
        prod = times(to_spectrum(whole[...], window), spec)
        sig = from_spectrum(high[: rest + HALO, :], *prod)
        put(yq, 0, rounded(g[:, lanes].astype(F32) * sig[:rest]), lanes.start)
        more_out[:, lanes] = sig[rest:]
    put(xq, 0, q[BLOCK - 2 * HALO :, :].astype(F32))
    for h, lanes in halves(width):
        next_out[:HALO, lanes] = yq[h, :HALO]
        next_out[HALO:, lanes] = yq[h, rest - HALO : rest]
        gq_out[:, lanes] = anticausal(yq, h, 0, rest, taps_of(w, 0, lanes)).astype(BF16)
        sums_out[:, lanes] = lag_sums(yq, 0, xq, 2 * HALO, h, rest, w.shape[1])


def third_kernel(
    me, k, v, tails, ends, ahead, gated, ggi, ks, vs, more, taps, w, spec, half, whole, low,
    gk_out, gv_out, next_out, sums_out, own_out, *rest_refs,
):
    *more_out, xe, xk, xv, yk, yv, acc, mscr = rest_refs
    rows, width = k.shape
    groups = spec.shape[2]
    rest = rows - BLOCK
    step = pl.program_id(0)
    count = w.shape[1]

    @pl.when(step == 0)
    def _():
        acc[...] = jnp.zeros_like(acc)

    head = ahead[: 4 * HALO, :].astype(F32)
    tail = tails[...].astype(F32)
    end = ends[...].astype(F32)
    for at in range(3):
        put(xe.at[at], HALO, end[at * HALO : (at + 1) * HALO])
        put(xe.at[at], 2 * HALO, head[at * HALO : (at + 1) * HALO])
        put(xe.at[at], 0, jnp.zeros((HALO, width), F32))
    news = [[], [], []]
    for h, lanes in halves(width):
        for at in range(3):
            news[at].append(causal(xe.at[at], h, 2 * HALO, HALO, taps_of(w, at, lanes)))
    qs_new, ks_new, vs_new = (jnp.concatenate(x, axis=1) for x in news)
    gated_new = rounded(ks_new * vs_new)
    ggi_new = head[3 * HALO :] * qs_new
    put(xe.at[0], HALO, gated_new)
    for h, lanes in halves(width):
        total = more[:, lanes]
        for j in range(HALO):
            at = lanes.start % groups
            total = total + taps[j : j + 1, at : at + LANES] * xe[0, h, HALO - j : 2 * HALO - j]
        next_out[:, lanes] = rounded(head[3 * HALO :, lanes] * total)
    put(xk, 0, tail[HALO : 2 * HALO])
    put(xk, HALO, k[...].astype(F32))
    put(xv, 0, tail[2 * HALO :])
    put(xv, HALO, v[...].astype(F32))
    fill = 3 * BLOCK - rows - HALO - BLOCK
    for lanes in blocks(width, groups):
        later = jnp.concatenate(
            [ggi_new[:, lanes], ahead[4 * HALO :, lanes].astype(F32), jnp.zeros((fill, groups), F32)],
            axis=0,
        ).astype(BF16)
        ggi_ext = jnp.concatenate([ggi[:, lanes], later], axis=0)
        own = jnp.concatenate([gated[:, lanes], jnp.zeros((WINDOW - rows, groups), BF16)], axis=0)
        for at in range(2):
            win = to_spectrum(whole[...], ggi_ext[at * BLOCK : at * BLOCK + WINDOW])
            gs = to_spectrum(half[...], own[at * BLOCK : (at + 1) * BLOCK])
            acc[0] += gs[:BLOCK] * win[:BLOCK]
            acc[1] += gs[BLOCK:] * win[BLOCK:]
            acc[2] += gs[:BLOCK] * win[BLOCK:] - gs[BLOCK:] * win[:BLOCK]
            prod = times_conj(win, spec)
            if at == 0:
                gg = from_spectrum(low[...], *prod)
                gk = (gg * vs[:BLOCK, lanes]).astype(BF16)
                gv = (gg * ks[:BLOCK, lanes]).astype(BF16)
                span = slice(0, BLOCK)
            else:
                gg = from_spectrum(low[: rest + HALO, :], *prod)
                zero = jnp.zeros((HALO, groups), F32)
                gk = jnp.concatenate(
                    [gg[:rest] * vs[BLOCK:, lanes], gg[rest:] * vs_new[:, lanes], zero], axis=0
                ).astype(BF16)
                gv = jnp.concatenate(
                    [gg[:rest] * ks[BLOCK:, lanes], gg[rest:] * ks_new[:, lanes], zero], axis=0
                ).astype(BF16)
                span = slice(BLOCK, rows + 2 * HALO)
            gk_out[span, lanes] = gk
            gv_out[span, lanes] = gv
            put(yk, span.start, gk.astype(F32), lanes.start)
            put(yv, span.start, gv.astype(F32), lanes.start)
        for h in range(lanes.start // LANES, lanes.stop // LANES):
            here = slice(h * LANES, (h + 1) * LANES)
            sums_out[:HALO, here] = lag_sums(yk, 0, xk, HALO, h, rows, count)
            sums_out[HALO:, here] = lag_sums(yv, 0, xv, HALO, h, rows, count)

    @pl.when(step == pl.num_programs(0) - 1)
    def _():
        first = lax.broadcasted_iota(jnp.int32, (BLOCK, groups), 0) == 0
        real = acc[0] + jnp.where(first, 0.0, acc[1])
        imag = jnp.where(first, acc[1], acc[2])
        mscr[...] = from_spectrum(low[...], real, imag).T
        mine = own_out.shape[0]
        share = groups // mine
        for at in range(share):
            part = mscr[pl.ds(pl.multiple_of(lax.rem(me[0] + at, share) * mine, mine), mine)]
            if at == 0:
                own_out[...] = part
            else:
                more_out[at - 1][...] = part.astype(BF16)


def fourth_kernel(gk, gv, near, far, w, gq_in, gk_out, gv_out, gq_out, yq, yk, yv):
    rows, width = gk_out.shape
    put(yk, 0, gk[...].astype(F32))
    put(yv, 0, gv[...].astype(F32))
    put(yq, 0, near[...])
    put(yq, HALO, far[...])
    put(yq, 2 * HALO, jnp.zeros((HALO, width), F32))
    old = gq_in[...].astype(F32)[:HALO]
    for h, lanes in halves(width):
        for i, ref, out in ((1, yk, gk_out), (2, yv, gv_out)):
            weights = taps_of(w, i, lanes)
            for at, size in pieces(rows):
                out[at : at + size, lanes] = anticausal(ref, h, at, size, weights).astype(BF16)
        fixed = anticausal(yq, h, 0, HALO, taps_of(w, 0, lanes))
        gq_out[:, lanes] = jnp.concatenate([old[:, lanes], fixed], axis=0).astype(BF16)


def pack_kernel(sums, own, *refs):
    *parts, late_out, send_out = refs
    total = own[...]
    for part in parts:
        total = total + part[...].astype(F32)
    spread = halves(sums.shape[1])
    count = total.shape[0] // len(spread)
    late_out[: 2 * HALO] = sums[...]
    for h, lanes in spread:
        late_out[2 * HALO :, lanes] = total[h * count : (h + 1) * count]
    send_out[...] = late_out[...].astype(BF16)


def fifth_kernel(
    q, tails, sums, g, gated, behind, spec, whole, high,
    yq_out, sums_out, send_out,
    xq, yq,
):
    width = q.shape[1]
    put(xq, 0, tails[...].astype(F32)[:HALO])
    put(xq, HALO, q[...].astype(F32))
    for lanes in blocks(width, spec.shape[2]):
        window = jnp.concatenate([behind[:, lanes], gated[:, lanes]], axis=0)
        sig = from_spectrum(high[...], *times(to_spectrum(whole[...], window), spec))
        grad = (g[:, lanes].astype(F32) * sig).astype(BF16)
        yq_out[:, lanes] = grad
        put(yq, 0, grad.astype(F32), lanes.start)
    for h, lanes in halves(width):
        sums_out[:, lanes] = sums[:, lanes] + lag_sums(yq, 0, xq, HALO, h, BLOCK, sums.shape[0] - 1)
    send_out[...] = sums_out[...].astype(BF16)


def sixth_kernel(grad, following, w, gq_in, gq_out, yq):
    put(yq, 0, grad[...].astype(F32))
    put(yq, BLOCK, following[...])
    for h, lanes in halves(grad.shape[1]):
        weights = taps_of(w, 0, lanes)
        for at, size in pieces(BLOCK):
            gq_out[at : at + size, lanes] = anticausal(yq, h, at, size, weights).astype(BF16)


def shift(value, axis, steps):
    count = lax.axis_size(axis)
    initial, last = (max(0, -steps), min(count, count - steps))
    return lax.ppermute(value, axis, [(s, s + steps) for s in range(initial, last)])


def exchanged(sends, axis):
    count = lax.axis_size(axis)
    return [
        lax.ppermute(part, axis, [(s, (s + step) % count) for s in range(count)])
        for step, part in enumerate(sends, 1)
    ]


def swap(value, axis, bit):
    count = lax.axis_size(axis)
    return lax.ppermute(value, axis, [(s, s ^ (1 << bit)) for s in range(count)])


def sums_over(early, sent_early, late, sent_late, axis):
    count = lax.axis_size(axis)
    if count & (count - 1):
        return lax.psum(early, axis), lax.psum(late, axis)
    bits = count.bit_length() - 1
    alone = 1 * bits // 4
    for bit in range(bits - 1, bits - 1 - alone, -1):
        early = early + swap(sent_early, axis, bit).astype(F32)
        sent_early = early.astype(BF16)
    total = jnp.concatenate([early, late], axis=0)
    sent = jnp.concatenate([sent_early, sent_late], axis=0)
    for bit in range(bits - alone):
        total = total + swap(sent, axis, bit).astype(F32)
        sent = total.astype(BF16)
    early, late = total[: early.shape[0]], total[early.shape[0] :]
    sent = late.astype(BF16)
    for bit in range(bits - alone, bits):
        late = late + swap(sent, axis, bit).astype(F32)
        sent = late.astype(BF16)
    return early, late


def in_hbm(value):
    return pltpu.with_memory_space_constraint(value, pltpu.HBM)


def shards(query, key, value, grad_out, short_filter, medium_filter):
    rows, channels = query.shape
    groups = medium_filter.shape[0] * lax.axis_size("fsdp")
    width = groups
    rest = rows - BLOCK
    taps_short = short_filter.shape[1]
    whole, half, low, high = (jnp.asarray(m) for m in transforms())

    def col(count, at=0, wide=width):
        return pl.BlockSpec((count, wide), lambda i: (at, i))

    def filters(wide=width):
        return pl.BlockSpec((3, taps_short, wide), lambda i: (0, 0, i))

    def out(count, dtype):
        return jax.ShapeDtypeStruct((count, channels), dtype)

    def scratch(count, wide=width):
        return pltpu.VMEM((wide // LANES, count, LANES), F32)

    def cost(flops, moved):
        return pl.CostEstimate(flops=int(flops), bytes_accessed=int(moved), transcendentals=0)

    query, key, value, grad_out, short_filter = (
        in_hbm(x) for x in (query, key, value, grad_out, short_filter)
    )
    whole, half, low, high = (in_hbm(x) for x in (whole, half, low, high))
    room = pltpu.CompilerParams(vmem_limit_bytes=ROOM)
    wide = min(4 * width, channels)
    pair = min(2 * width, channels)
    last = rows // (2 * HALO) - 1
    ends, ahead = pl.pallas_call(
        first_kernel,
        grid=(channels // wide,),
        in_specs=[col(BLOCK + 2 * HALO, 0, wide)] * 2
        + [col(2 * HALO, last, wide)] * 3
        + [col(2 * HALO, 0, wide)] * 2
        + [filters(wide)],
        out_specs=[col(3 * HALO, 0, wide), col(BLOCK + 4 * HALO, 0, wide)],
        out_shape=[out(3 * HALO, BF16), out(BLOCK + 4 * HALO, BF16)],
        scratch_shapes=[scratch(BLOCK + 2 * HALO, wide)],
        name="first",
        compiler_params=room,
    )(query, grad_out, query, key, value, key, value, short_filter)
    tails = shift(ends, "seq", 1)
    ahead = shift(ahead, "seq", -1)
    share = lax.axis_size("fsdp")
    taps = exchanged([medium_filter.astype(BF16)] * (share - 1), "fsdp")

    gated, ggi, ks, vs, behind = pl.pallas_call(
        second_kernel,
        grid=(channels // wide,),
        in_specs=[col(rows, 0, wide)] * 4 + [col(3 * HALO, 0, wide), filters(wide)],
        out_specs=[col(rows, 0, wide)] * 4 + [col(BLOCK, 0, wide)],
        out_shape=[
            out(rows, BF16), out(rows, BF16), out(rows, F32), out(rows, F32), out(BLOCK, BF16),
        ],
        scratch_shapes=[scratch(rows + HALO, wide)] * 3,
        cost_estimate=cost(4e9, 20e6),
        name="second",
        compiler_params=room,
    )(query, key, value, grad_out, tails, short_filter)
    behind = shift(behind, "seq", 1)

    me = lax.axis_index("fsdp").astype(jnp.int32).reshape(1)
    many = channels // wide

    def big(count, at=0):
        return pl.BlockSpec((count, wide), lambda i, *_: (at, i))

    def two(count, at=0):
        return pl.BlockSpec((count, pair), lambda i, *_: (at, i))

    def still(shape):
        return pl.BlockSpec(shape, lambda i, *_: (0,) * len(shape))

    two_filters = pl.BlockSpec((3, taps_short, pair), lambda i, *_: (0, 0, i))
    big_filters = pl.BlockSpec((3, taps_short, wide), lambda i, *_: (0, 0, i))
    corner = BLOCK // rest
    edge_block = rows // (2 * HALO) - 1
    grad_query, nexts, sums_q, more, spec, tap_rows = pl.pallas_call(
        middle_kernel,
        grid_spec=pltpu.PrefetchScalarGridSpec(
            num_scalar_prefetch=1,
            grid=(many,),
            in_specs=[big(rows), big(rest, corner), big(rows), big_filters]
            + [still(m.shape) for m in (half, whole, high)]
            + [still(medium_filter.shape)] * share,
            out_specs=[big(rest, corner), big(2 * HALO), big(HALO), big(HALO)]
            + [still((3, BLOCK, width)), still((HALO, width))],
            scratch_shapes=[scratch(rest + 2 * HALO, wide)] * 2
            + [pltpu.VMEM((3, BLOCK, width), F32), pltpu.VMEM((width, BLOCK), F32)],
        ),
        out_shape=[
            out(rows, BF16), out(2 * HALO, F32), out(HALO, F32), out(HALO, F32),
            jax.ShapeDtypeStruct((3, BLOCK, width), F32), jax.ShapeDtypeStruct((HALO, width), F32),
        ],
        cost_estimate=cost(4e9, 8e6),
        name="middle",
        compiler_params=room,
    )(me, query, grad_out, gated, short_filter, half, whole, high, medium_filter, *taps)

    mine = (width // share, BLOCK)
    gk, gv, far, sums_kv, own, *sends = pl.pallas_call(
        third_kernel,
        grid_spec=pltpu.PrefetchScalarGridSpec(
            num_scalar_prefetch=1,
            grid=(channels // pair,),
            in_specs=[two(rows)] * 2
            + [two(3 * HALO)] * 2
            + [two(BLOCK + 4 * HALO)]
            + [two(rows)] * 4
            + [two(HALO), still(tap_rows.shape), two_filters, still((3, BLOCK, width))]
            + [still(m.shape) for m in (half, whole, low)],
            out_specs=[two(rows + 2 * HALO)] * 2
            + [two(HALO)]
            + [two(2 * HALO)]
            + [still(mine)] * share,
            scratch_shapes=[pltpu.VMEM((3, pair // LANES, 3 * HALO, LANES), F32)]
            + [scratch(rows + 2 * HALO, pair)] * 4
            + [pltpu.VMEM((3, BLOCK, width), F32), pltpu.VMEM((width, BLOCK), F32)],
        ),
        out_shape=[out(rows + 2 * HALO, BF16)] * 2
        + [out(HALO, F32), out(2 * HALO, F32)]
        + [jax.ShapeDtypeStruct(mine, F32)]
        + [jax.ShapeDtypeStruct(mine, BF16)] * (share - 1),
        cost_estimate=cost(8e9, 20e6),
        name="third",
        compiler_params=room,
    )(me, key, value, tails, ends, ahead, gated, ggi, ks, vs, more, tap_rows,
      short_filter, spec, half, whole, low)
    parts = exchanged(sends, "fsdp")

    grad_key, grad_value, grad_query = pl.pallas_call(
        fourth_kernel,
        grid=(many,),
        in_specs=[big(rows + 2 * HALO)] * 2
        + [big(HALO, 1), big(HALO), big_filters, big(2 * HALO, edge_block)],
        out_specs=[big(rows), big(rows), big(2 * HALO, edge_block)],
        out_shape=[out(rows, BF16)] * 3,
        scratch_shapes=[scratch(3 * HALO, wide)] + [scratch(rows + 2 * HALO, wide)] * 2,
        input_output_aliases={5: 2},
        cost_estimate=cost(4e9, 10e6),
        name="fourth",
        compiler_params=room,
    )(gk, gv, nexts, far, short_filter, grad_query)

    extra = mine[0] * BLOCK // channels
    tall = (2 * HALO + extra, channels)
    sums_kv, sent_kv = pl.pallas_call(
        pack_kernel,
        out_shape=[jax.ShapeDtypeStruct(tall, F32), jax.ShapeDtypeStruct(tall, BF16)],
        name="pack",
        compiler_params=room,
    )(sums_kv, own, *parts)

    grads, sums_q, sent_q = pl.pallas_call(
        fifth_kernel,
        grid=(many,),
        in_specs=[big(BLOCK), big(3 * HALO), big(HALO)]
        + [big(BLOCK)] * 3
        + [still((3, BLOCK, width)), still(whole.shape), still(high.shape)],
        out_specs=[big(BLOCK), big(HALO), big(HALO)],
        out_shape=[out(BLOCK, BF16), out(HALO, F32), out(HALO, BF16)],
        scratch_shapes=[scratch(BLOCK + HALO, wide)] * 2,
        cost_estimate=cost(2e9, 8e6),
        name="fifth",
        compiler_params=room,
    )(query, tails, sums_q, grad_out, gated, behind, spec, whole, high)

    grad_query = pl.pallas_call(
        sixth_kernel,
        grid=(many,),
        in_specs=[big(BLOCK), big(HALO), big_filters, pl.BlockSpec(memory_space=pl.ANY)],
        out_specs=big(BLOCK),
        out_shape=out(rows, BF16),
        scratch_shapes=[scratch(BLOCK + HALO, wide)],
        input_output_aliases={3: 0},
        cost_estimate=cost(2e9, 3e6),
        name="sixth",
        compiler_params=room,
    )(grads, nexts, short_filter, grad_query)

    early, late = sums_over(sums_kv, sent_kv, sums_q, sent_q, "seq")
    packed = early[2 * HALO :]
    grad_medium = jnp.concatenate(
        [packed[:, at : at + BLOCK] for at in range(0, channels, BLOCK)], axis=0
    )
    grad_short = jnp.stack([late[:taps_short], early[:taps_short], early[HALO : HALO + taps_short]])
    return grad_query, grad_key, grad_value, grad_short, grad_medium


def solution(mesh):
    in_specs = (
        P("seq", "fsdp"),
        P("seq", "fsdp"),
        P("seq", "fsdp"),
        P("seq", "fsdp"),
        P(None, None, "fsdp"),
        P("fsdp", None),
    )
    out_specs = (
        P("seq", "fsdp"),
        P("seq", "fsdp"),
        P("seq", "fsdp"),
        P(None, None, "fsdp"),
        P("fsdp", None),
    )
    return jax.shard_map(shards, mesh=mesh, in_specs=in_specs, out_specs=out_specs, check_vma=False)
```

```python
import numpy as np
import jax
import jax.numpy as jnp
from jax import lax
from jax.experimental import pallas as pl
from jax.experimental.pallas import tpu as pltpu
from jax.sharding import PartitionSpec as P


HALO = 8
BLOCK = 128
WINDOW = 2 * BLOCK
F32 = jnp.float32
BF16 = jnp.bfloat16


def split_terms(matrix):
    high = matrix.astype(BF16)
    low = (matrix - high.astype(np.float32)).astype(BF16)
    return np.asarray(high), np.asarray(low)


def transforms():
    time = np.arange(WINDOW)
    freq = np.arange(BLOCK)
    angle = 2 * np.pi * ((freq[:, None] * time[None, :]) % WINDOW) / WINDOW
    cosine, sine = np.cos(angle), np.sin(angle)
    nyquist = np.where(time % 2 == 0, 1.0, -1.0)
    forward = np.concatenate([cosine, -sine]).astype(np.float64)
    forward[BLOCK] = nyquist
    scale = np.full(WINDOW, 2.0 / WINDOW)
    scale[0] = scale[BLOCK] = 1.0 / WINDOW
    inverse = forward.T * scale[None, :]
    f_high, f_low = split_terms(forward.astype(np.float32))
    i_high, i_low = split_terms(inverse.astype(np.float32))
    whole = np.concatenate([f_high, f_low], axis=1)
    half = np.concatenate([f_high[:, :BLOCK], f_low[:, :BLOCK]], axis=1)
    back = np.concatenate([i_high, i_low], axis=1)
    return whole, half, back[:BLOCK], back[BLOCK:]


def dot(left, right):
    return jnp.dot(left, right, preferred_element_type=F32)


def to_spectrum(matrix, rows):
    return dot(matrix, jnp.concatenate([rows, rows], axis=0))


def from_spectrum(matrix, real, imag):
    whole = jnp.concatenate([real, imag], axis=0).astype(BF16)
    return to_spectrum(matrix, whole)


def times(spec, taps):
    xr, xi = spec[:BLOCK], spec[BLOCK:]
    return xr * taps[0] - xi * taps[1], xr * taps[1] + xi * taps[2]


def times_conj(spec, taps):
    xr, xi = spec[:BLOCK], spec[BLOCK:]
    return xr * taps[0] + xi * taps[1], xi * taps[2] - xr * taps[1]


def blocks(wide, width):
    return [slice(at, at + width) for at in range(0, wide, width)]


def rounded(value):
    return value.astype(BF16).astype(F32)


LANES = 128
ROOM = 20 * 1024 * 1024
CHUNK = 64


def halves(width):
    return [(at // LANES, slice(at, at + LANES)) for at in range(0, width, LANES)]


def pieces(count):
    return [(at, min(CHUNK, count - at)) for at in range(0, count, CHUNK)]


def put(ref, at, value, lane=0):
    for h, lanes in halves(value.shape[1]):
        ref[h + lane // LANES, at : at + value.shape[0]] = value[:, lanes]


def causal(ref, h, at, count, weights):
    total = None
    for j, weight in enumerate(weights):
        term = weight * ref[h, at - j : at - j + count]
        total = term if total is None else total + term
    return total


def anticausal(ref, h, at, count, weights):
    total = None
    for j, weight in enumerate(weights):
        term = weight * ref[h, at + j : at + j + count]
        total = term if total is None else total + term
    return total


def taps_of(w, index, lanes):
    return [w[index, j : j + 1, lanes] for j in range(w.shape[1])]


def lag_sums(grad, g_at, x, x_at, h, count, taps):
    totals = [None] * taps
    for at, size in pieces(count):
        mine = grad[h, g_at + at : g_at + at + size]
        for j in range(taps):
            prod = mine * x[h, x_at + at - j : x_at + at - j + size]
            part = jnp.sum(prod.reshape(size // 8, 8, LANES), axis=0)
            totals[j] = part if totals[j] is None else totals[j] + part
    rows = [jnp.sum(t, axis=0, keepdims=True) for t in totals]
    return jnp.concatenate(rows + [jnp.zeros_like(rows[0])], axis=0)


def first_kernel(q, g, q_tail, k_tail, v_tail, k_head, v_head, w, tails, ahead, xq):
    tails[...] = jnp.concatenate(
        [x[...].astype(F32)[HALO:] for x in (q_tail, k_tail, v_tail)], axis=0
    ).astype(BF16)
    put(xq, 0, q[...].astype(F32))
    grad = g[...].astype(F32)
    heads = [x[: 2 * HALO, :].astype(F32)[:HALO] for x in (q, k_head, v_head, g)]
    ahead[: 4 * HALO] = jnp.concatenate(heads, axis=0).astype(BF16)
    for h, lanes in halves(q.shape[1]):
        weights = taps_of(w, 0, lanes)
        for at, size in pieces(BLOCK):
            qs = causal(xq, h, HALO + at, size, weights)
            ahead[4 * HALO + at : 4 * HALO + at + size, lanes] = (
                grad[HALO + at : HALO + at + size, lanes] * qs
            ).astype(BF16)


def second_kernel(
    q, k, v, g, tails, w,
    gated_out, ggi_out, ks_out, vs_out, behind_out,
    xq, xk, xv,
):
    rows, width = q.shape
    tail = tails[...].astype(F32)
    for at, (ref, x) in enumerate(((xq, q), (xk, k), (xv, v))):
        put(ref, 0, tail[at * HALO : (at + 1) * HALO])
        put(ref, HALO, x[...].astype(F32))
    for h, lanes in halves(width):
        wq, wk, wv = (taps_of(w, i, lanes) for i in range(3))
        for at, size in pieces(rows):
            span = slice(at, at + size)
            ks = causal(xk, h, HALO + at, size, wk)
            vs = causal(xv, h, HALO + at, size, wv)
            ks_out[span, lanes] = ks
            vs_out[span, lanes] = vs
            gated_out[span, lanes] = (ks * vs).astype(BF16)
            qs = causal(xq, h, HALO + at, size, wq)
            ggi_out[span, lanes] = (g[span, lanes].astype(F32) * qs).astype(BF16)
    behind_out[...] = gated_out[rows - BLOCK :, :]


def middle_kernel(me, _, q, g, gated, w, half, whole, high, own_taps, *refs):
    *more_taps, gq_out, next_out, sums_out, more_out, spec_out, rows_out, xq, yq, spec, taps = refs
    rows, width = gated.shape
    rest = rows - BLOCK
    groups = taps.shape[0]

    @pl.when(pl.program_id(0) == 0)
    def _():
        mine = own_taps.shape[0]
        share = groups // mine
        for at, part in enumerate([own_taps] + more_taps):
            start = lax.rem(me[0] + share - at, share) * mine
            taps[pl.ds(pl.multiple_of(start, mine), mine)] = part[...].astype(BF16).astype(F32)
        whole_taps = taps[...].astype(BF16)
        both = jnp.concatenate([whole_taps, whole_taps], axis=1)
        whole_spec = lax.dot_general(
            half[...], both, (((1,), (1,)), ((), ())), preferred_element_type=F32
        )
        real, imag = whole_spec[:BLOCK], whole_spec[BLOCK:]
        first = lax.broadcasted_iota(jnp.int32, real.shape, 0) == 0
        spec[0] = real
        spec[1] = jnp.where(first, 0.0, imag)
        spec[2] = jnp.where(first, imag, real)
        spec_out[...] = spec[...]
        rows_out[...] = taps[...].T[:HALO]

    for lanes in blocks(width, groups):
        pad = jnp.zeros((WINDOW - rows, groups), BF16)
        window = jnp.concatenate([gated[:, lanes], pad], axis=0)
        prod = times(to_spectrum(whole[...], window), spec)
        sig = from_spectrum(high[: rest + HALO, :], *prod)
        put(yq, 0, rounded(g[:, lanes].astype(F32) * sig[:rest]), lanes.start)
        more_out[:, lanes] = sig[rest:]
    put(xq, 0, q[BLOCK - 2 * HALO :, :].astype(F32))
    for h, lanes in halves(width):
        next_out[:HALO, lanes] = yq[h, :HALO]
        next_out[HALO:, lanes] = yq[h, rest - HALO : rest]
        gq_out[:, lanes] = anticausal(yq, h, 0, rest, taps_of(w, 0, lanes)).astype(BF16)
        sums_out[:, lanes] = lag_sums(yq, 0, xq, 2 * HALO, h, rest, w.shape[1])


def third_kernel(
    me, k, v, tails, ends, ahead, gated, ggi, ks, vs, more, taps, w, spec, half, whole, low,
    gk_out, gv_out, next_out, sums_out, own_out, *rest_refs,
):
    *more_out, xe, xk, xv, yk, yv, acc, mscr = rest_refs
    rows, width = k.shape
    groups = spec.shape[2]
    rest = rows - BLOCK
    step = pl.program_id(0)
    count = w.shape[1]

    @pl.when(step == 0)
    def _():
        acc[...] = jnp.zeros_like(acc)

    head = ahead[: 4 * HALO, :].astype(F32)
    tail = tails[...].astype(F32)
    end = ends[...].astype(F32)
    for at in range(3):
        put(xe.at[at], HALO, end[at * HALO : (at + 1) * HALO])
        put(xe.at[at], 2 * HALO, head[at * HALO : (at + 1) * HALO])
        put(xe.at[at], 0, jnp.zeros((HALO, width), F32))
    news = [[], [], []]
    for h, lanes in halves(width):
        for at in range(3):
            news[at].append(causal(xe.at[at], h, 2 * HALO, HALO, taps_of(w, at, lanes)))
    qs_new, ks_new, vs_new = (jnp.concatenate(x, axis=1) for x in news)
    gated_new = rounded(ks_new * vs_new)
    ggi_new = head[3 * HALO :] * qs_new
    put(xe.at[0], HALO, gated_new)
    for h, lanes in halves(width):
        total = more[:, lanes]
        for j in range(HALO):
            at = lanes.start % groups
            total = total + taps[j : j + 1, at : at + LANES] * xe[0, h, HALO - j : 2 * HALO - j]
        next_out[:, lanes] = rounded(head[3 * HALO :, lanes] * total)
    put(xk, 0, tail[HALO : 2 * HALO])
    put(xk, HALO, k[...].astype(F32))
    put(xv, 0, tail[2 * HALO :])
    put(xv, HALO, v[...].astype(F32))
    fill = 3 * BLOCK - rows - HALO - BLOCK
    for lanes in blocks(width, groups):
        later = jnp.concatenate(
            [ggi_new[:, lanes], ahead[4 * HALO :, lanes].astype(F32), jnp.zeros((fill, groups), F32)],
            axis=0,
        ).astype(BF16)
        ggi_ext = jnp.concatenate([ggi[:, lanes], later], axis=0)
        own = jnp.concatenate([gated[:, lanes], jnp.zeros((WINDOW - rows, groups), BF16)], axis=0)
        for at in range(2):
            win = to_spectrum(whole[...], ggi_ext[at * BLOCK : at * BLOCK + WINDOW])
            gs = to_spectrum(half[...], own[at * BLOCK : (at + 1) * BLOCK])
            acc[0] += gs[:BLOCK] * win[:BLOCK]
            acc[1] += gs[BLOCK:] * win[BLOCK:]
            acc[2] += gs[:BLOCK] * win[BLOCK:] - gs[BLOCK:] * win[:BLOCK]
            prod = times_conj(win, spec)
            if at == 0:
                gg = from_spectrum(low[...], *prod)
                gk = (gg * vs[:BLOCK, lanes]).astype(BF16)
                gv = (gg * ks[:BLOCK, lanes]).astype(BF16)
                span = slice(0, BLOCK)
            else:
                gg = from_spectrum(low[: rest + HALO, :], *prod)
                zero = jnp.zeros((HALO, groups), F32)
                gk = jnp.concatenate(
                    [gg[:rest] * vs[BLOCK:, lanes], gg[rest:] * vs_new[:, lanes], zero], axis=0
                ).astype(BF16)
                gv = jnp.concatenate(
                    [gg[:rest] * ks[BLOCK:, lanes], gg[rest:] * ks_new[:, lanes], zero], axis=0
                ).astype(BF16)
                span = slice(BLOCK, rows + 2 * HALO)
            gk_out[span, lanes] = gk
            gv_out[span, lanes] = gv
            put(yk, span.start, gk.astype(F32), lanes.start)
            put(yv, span.start, gv.astype(F32), lanes.start)
        for h in range(lanes.start // LANES, lanes.stop // LANES):
            here = slice(h * LANES, (h + 1) * LANES)
            sums_out[:HALO, here] = lag_sums(yk, 0, xk, HALO, h, rows, count)
            sums_out[HALO:, here] = lag_sums(yv, 0, xv, HALO, h, rows, count)

    @pl.when(step == pl.num_programs(0) - 1)
    def _():
        first = lax.broadcasted_iota(jnp.int32, (BLOCK, groups), 0) == 0
        real = acc[0] + jnp.where(first, 0.0, acc[1])
        imag = jnp.where(first, acc[1], acc[2])
        mscr[...] = from_spectrum(low[...], real, imag).T
        mine = own_out.shape[0]
        share = groups // mine
        for at in range(share):
            part = mscr[pl.ds(pl.multiple_of(lax.rem(me[0] + at, share) * mine, mine), mine)]
            if at == 0:
                own_out[...] = part
            else:
                more_out[at - 1][...] = part.astype(BF16)


def fourth_kernel(gk, gv, near, far, w, gq_in, gk_out, gv_out, gq_out, yq, yk, yv):
    rows, width = gk_out.shape
    put(yk, 0, gk[...].astype(F32))
    put(yv, 0, gv[...].astype(F32))
    put(yq, 0, near[...])
    put(yq, HALO, far[...])
    put(yq, 2 * HALO, jnp.zeros((HALO, width), F32))
    old = gq_in[...].astype(F32)[:HALO]
    for h, lanes in halves(width):
        for i, ref, out in ((1, yk, gk_out), (2, yv, gv_out)):
            weights = taps_of(w, i, lanes)
            for at, size in pieces(rows):
                out[at : at + size, lanes] = anticausal(ref, h, at, size, weights).astype(BF16)
        fixed = anticausal(yq, h, 0, HALO, taps_of(w, 0, lanes))
        gq_out[:, lanes] = jnp.concatenate([old[:, lanes], fixed], axis=0).astype(BF16)


def pack_kernel(place, sums, own, *refs):
    *parts, keep_out, send_out, both = refs
    total = own[...]
    for part in parts:
        total = total + part[...].astype(F32)
    spread = halves(sums.shape[1])
    count = total.shape[0] // len(spread)
    both[: 2 * HALO] = sums[...]
    for h, lanes in spread:
        both[2 * HALO :, lanes] = total[h * count : (h + 1) * count]
    middle = sums.shape[1] // 2
    left, right = both[:, :middle], both[:, middle:]
    lower = lax.rem(place[0], 2) == 0
    keep_out[...] = jnp.where(lower, left, right)
    send_out[...] = jnp.where(lower, right, left).astype(BF16)


def fifth_kernel(
    q, tails, sums, g, gated, behind, spec, lead, back,
    yq_out, sums_out, send_out,
    xq, yq,
):
    width = q.shape[1]
    put(xq, 0, tails[...].astype(F32)[:HALO])
    put(xq, HALO, q[...].astype(F32))
    for lanes in blocks(width, spec.shape[2]):
        window = jnp.concatenate([behind[:, lanes], gated[:, lanes]], axis=0)
        prod = jnp.concatenate(times(dot(lead[...], window), spec), axis=0)
        sig = dot(back[...], prod.astype(BF16))
        grad = (g[:, lanes].astype(F32) * sig).astype(BF16)
        yq_out[:, lanes] = grad
        put(yq, 0, grad.astype(F32), lanes.start)
    for h, lanes in halves(width):
        sums_out[:, lanes] = sums[:, lanes] + lag_sums(yq, 0, xq, HALO, h, BLOCK, sums.shape[0] - 1)
    send_out[...] = sums_out[...].astype(BF16)


def sixth_kernel(grad, following, w, gq_in, gq_out, yq):
    put(yq, 0, grad[...].astype(F32))
    put(yq, BLOCK, following[...])
    for h, lanes in halves(grad.shape[1]):
        weights = taps_of(w, 0, lanes)
        for at, size in pieces(BLOCK):
            gq_out[at : at + size, lanes] = anticausal(yq, h, at, size, weights).astype(BF16)


def last_kernel(place, total, other, short_out, medium_out):
    lower = lax.rem(place[0], 2) == 0
    middle = total.shape[1]
    taps = short_out.shape[1]
    rows = total.shape[0] - 2 * HALO
    mine, theirs = total[...], other[...].astype(F32)
    late = mine[rows:] + theirs[rows:]
    sides = (
        jnp.where(lower, mine[:rows], theirs[:rows]),
        jnp.where(lower, theirs[:rows], mine[:rows]),
    )
    for at, part in enumerate(sides):
        here = slice(at * middle, (at + 1) * middle)
        short_out[0, :, here] = late[at * HALO : at * HALO + taps]
        short_out[1, :, here] = part[:taps]
        short_out[2, :, here] = part[HALO : HALO + taps]
        spread = halves(middle)
        count = rows - 2 * HALO
        for h, lanes in spread:
            place = (at * len(spread) + h) * count
            medium_out[place : place + count] = part[2 * HALO :, lanes]


def shift(value, axis, steps):
    count = lax.axis_size(axis)
    initial, last = (max(0, -steps), min(count, count - steps))
    return lax.ppermute(value, axis, [(s, s + steps) for s in range(initial, last)])


def exchanged(sends, axis):
    count = lax.axis_size(axis)
    return [
        lax.ppermute(part, axis, [(s, (s + step) % count) for s in range(count)])
        for step, part in enumerate(sends, 1)
    ]


def swap(value, axis, bit):
    count = lax.axis_size(axis)
    return lax.ppermute(value, axis, [(s, s ^ (1 << bit)) for s in range(count)])


def sums_over(kept, sent, late, sent_late, axis):
    count = lax.axis_size(axis)
    bits = count.bit_length() - 1
    middle = late.shape[1] // 2

    def stacked(value):
        return jnp.concatenate([value[:, :middle], value[:, middle:]], axis=0)

    early = kept + swap(sent, axis, 0).astype(F32)
    total = jnp.concatenate([early, stacked(late)], axis=0)
    sent = jnp.concatenate([early.astype(BF16), stacked(sent_late)], axis=0)
    for bit in range(bits - 1, 0, -1):
        total = total + swap(sent, axis, bit).astype(F32)
        sent = total.astype(BF16)
    return total, swap(sent, axis, 0)


def in_hbm(value):
    return pltpu.with_memory_space_constraint(value, pltpu.HBM)


def shards(query, key, value, grad_out, short_filter, medium_filter):
    rows, channels = query.shape
    groups = medium_filter.shape[0] * lax.axis_size("fsdp")
    width = groups
    rest = rows - BLOCK
    taps_short = short_filter.shape[1]
    matrices = transforms()
    whole, half, low, high = (jnp.asarray(m) for m in matrices)
    lead, back = (jnp.asarray(m[:, :WINDOW].copy()) for m in (matrices[0], matrices[3]))

    def col(count, at=0, wide=width):
        return pl.BlockSpec((count, wide), lambda i: (at, i))

    def filters(wide=width):
        return pl.BlockSpec((3, taps_short, wide), lambda i: (0, 0, i))

    def out(count, dtype):
        return jax.ShapeDtypeStruct((count, channels), dtype)

    def scratch(count, wide=width):
        return pltpu.VMEM((wide // LANES, count, LANES), F32)

    def cost(flops, moved):
        return pl.CostEstimate(flops=int(flops), bytes_accessed=int(moved), transcendentals=0)

    query, key, value, grad_out, short_filter = (
        in_hbm(x) for x in (query, key, value, grad_out, short_filter)
    )
    whole, half, low, high = (in_hbm(x) for x in (whole, half, low, high))
    room = pltpu.CompilerParams(vmem_limit_bytes=ROOM)
    wide = min(4 * width, channels)
    pair = min(2 * width, channels)
    last = rows // (2 * HALO) - 1
    ends, ahead = pl.pallas_call(
        first_kernel,
        grid=(channels // wide,),
        in_specs=[col(BLOCK + 2 * HALO, 0, wide)] * 2
        + [col(2 * HALO, last, wide)] * 3
        + [col(2 * HALO, 0, wide)] * 2
        + [filters(wide)],
        out_specs=[col(3 * HALO, 0, wide), col(BLOCK + 4 * HALO, 0, wide)],
        out_shape=[out(3 * HALO, BF16), out(BLOCK + 4 * HALO, BF16)],
        scratch_shapes=[scratch(BLOCK + 2 * HALO, wide)],
        name="first",
        compiler_params=room,
    )(query, grad_out, query, key, value, key, value, short_filter)
    tails = shift(ends, "seq", 1)
    ahead = shift(ahead, "seq", -1)
    share = lax.axis_size("fsdp")
    taps = exchanged([medium_filter.astype(BF16)] * (share - 1), "fsdp")

    gated, ggi, ks, vs, behind = pl.pallas_call(
        second_kernel,
        grid=(channels // wide,),
        in_specs=[col(rows, 0, wide)] * 4 + [col(3 * HALO, 0, wide), filters(wide)],
        out_specs=[col(rows, 0, wide)] * 4 + [col(BLOCK, 0, wide)],
        out_shape=[
            out(rows, BF16), out(rows, BF16), out(rows, F32), out(rows, F32), out(BLOCK, BF16),
        ],
        scratch_shapes=[scratch(rows + HALO, wide)] * 3,
        cost_estimate=cost(4e9, 20e6),
        name="second",
        compiler_params=room,
    )(query, key, value, grad_out, tails, short_filter)
    behind = shift(behind, "seq", 1)

    me = lax.axis_index("fsdp").astype(jnp.int32).reshape(1)
    place = lax.axis_index("seq").astype(jnp.int32).reshape(1)
    many = channels // wide

    def big(count, at=0):
        return pl.BlockSpec((count, wide), lambda i, *_: (at, i))

    def two(count, at=0):
        return pl.BlockSpec((count, pair), lambda i, *_: (at, i))

    def still(shape):
        return pl.BlockSpec(shape, lambda i, *_: (0,) * len(shape))

    two_filters = pl.BlockSpec((3, taps_short, pair), lambda i, *_: (0, 0, i))
    big_filters = pl.BlockSpec((3, taps_short, wide), lambda i, *_: (0, 0, i))
    corner = BLOCK // rest
    edge_block = rows // (2 * HALO) - 1
    grad_query, nexts, sums_q, more, spec, tap_rows = pl.pallas_call(
        middle_kernel,
        grid_spec=pltpu.PrefetchScalarGridSpec(
            num_scalar_prefetch=2,
            grid=(many,),
            in_specs=[big(rows), big(rest, corner), big(rows), big_filters]
            + [still(m.shape) for m in (half, whole, high)]
            + [still(medium_filter.shape)] * share,
            out_specs=[big(rest, corner), big(2 * HALO), big(HALO), big(HALO)]
            + [still((3, BLOCK, width)), still((HALO, width))],
            scratch_shapes=[scratch(rest + 2 * HALO, wide)] * 2
            + [pltpu.VMEM((3, BLOCK, width), F32), pltpu.VMEM((width, BLOCK), F32)],
        ),
        out_shape=[
            out(rows, BF16), out(2 * HALO, F32), out(HALO, F32), out(HALO, F32),
            jax.ShapeDtypeStruct((3, BLOCK, width), F32), jax.ShapeDtypeStruct((HALO, width), F32),
        ],
        cost_estimate=cost(4e9, 8e6),
        name="middle",
        compiler_params=room,
    )(me, place, query, grad_out, gated, short_filter, half, whole, high, medium_filter, *taps)

    mine = (width // share, BLOCK)
    gk, gv, far, sums_kv, own, *sends = pl.pallas_call(
        third_kernel,
        grid_spec=pltpu.PrefetchScalarGridSpec(
            num_scalar_prefetch=1,
            grid=(channels // pair,),
            in_specs=[two(rows)] * 2
            + [two(3 * HALO)] * 2
            + [two(BLOCK + 4 * HALO)]
            + [two(rows)] * 4
            + [two(HALO), still(tap_rows.shape), two_filters, still((3, BLOCK, width))]
            + [still(m.shape) for m in (half, whole, low)],
            out_specs=[two(rows + 2 * HALO)] * 2
            + [two(HALO)]
            + [two(2 * HALO)]
            + [still(mine)] * share,
            scratch_shapes=[pltpu.VMEM((3, pair // LANES, 3 * HALO, LANES), F32)]
            + [scratch(rows + 2 * HALO, pair)] * 4
            + [pltpu.VMEM((3, BLOCK, width), F32), pltpu.VMEM((width, BLOCK), F32)],
        ),
        out_shape=[out(rows + 2 * HALO, BF16)] * 2
        + [out(HALO, F32), out(2 * HALO, F32)]
        + [jax.ShapeDtypeStruct(mine, F32)]
        + [jax.ShapeDtypeStruct(mine, BF16)] * (share - 1),
        cost_estimate=cost(8e9, 20e6),
        name="third",
        compiler_params=room,
    )(me, key, value, tails, ends, ahead, gated, ggi, ks, vs, more, tap_rows,
      short_filter, spec, half, whole, low)
    parts = exchanged(sends, "fsdp")

    grad_key, grad_value, grad_query = pl.pallas_call(
        fourth_kernel,
        grid=(many,),
        in_specs=[big(rows + 2 * HALO)] * 2
        + [big(HALO, 1), big(HALO), big_filters, big(2 * HALO, edge_block)],
        out_specs=[big(rows), big(rows), big(2 * HALO, edge_block)],
        out_shape=[out(rows, BF16)] * 3,
        scratch_shapes=[scratch(3 * HALO, wide)] + [scratch(rows + 2 * HALO, wide)] * 2,
        input_output_aliases={5: 2},
        cost_estimate=cost(4e9, 10e6),
        name="fourth",
        compiler_params=room,
    )(gk, gv, nexts, far, short_filter, grad_query)

    extra = mine[0] * BLOCK // channels
    tall = (2 * HALO + extra, channels // 2)
    kept, sent = pl.pallas_call(
        pack_kernel,
        grid_spec=pltpu.PrefetchScalarGridSpec(
            num_scalar_prefetch=1,
            grid=(1,),
            in_specs=[still((2 * HALO, channels))] + [still(mine)] * share,
            out_specs=[still(tall)] * 2,
            scratch_shapes=[pltpu.VMEM((2 * HALO + extra, channels), F32)],
        ),
        out_shape=[jax.ShapeDtypeStruct(tall, F32), jax.ShapeDtypeStruct(tall, BF16)],
        name="pack",
        compiler_params=room,
    )(place, sums_kv, own, *parts)

    grads, sums_q, sent_q = pl.pallas_call(
        fifth_kernel,
        grid=(many,),
        in_specs=[big(BLOCK), big(3 * HALO), big(HALO)]
        + [big(BLOCK)] * 3
        + [still((3, BLOCK, width)), still(lead.shape), still(back.shape)],
        out_specs=[big(BLOCK), big(HALO), big(HALO)],
        out_shape=[out(BLOCK, BF16), out(HALO, F32), out(HALO, BF16)],
        scratch_shapes=[scratch(BLOCK + HALO, wide)] * 2,
        cost_estimate=cost(2e9, 8e6),
        name="fifth",
        compiler_params=room,
    )(query, tails, sums_q, grad_out, gated, behind, spec, lead, back)

    grad_query = pl.pallas_call(
        sixth_kernel,
        grid=(many,),
        in_specs=[big(BLOCK), big(HALO), big_filters, pl.BlockSpec(memory_space=pl.ANY)],
        out_specs=big(BLOCK),
        out_shape=out(rows, BF16),
        scratch_shapes=[scratch(BLOCK + HALO, wide)],
        input_output_aliases={3: 0},
        cost_estimate=cost(2e9, 3e6),
        name="sixth",
        compiler_params=room,
    )(grads, nexts, short_filter, grad_query)

    total, other = sums_over(kept, sent, sums_q, sent_q, "seq")
    grad_short, grad_medium = pl.pallas_call(
        last_kernel,
        grid_spec=pltpu.PrefetchScalarGridSpec(
            num_scalar_prefetch=1,
            grid=(1,),
            in_specs=[still(total.shape)] * 2,
            out_specs=[still(short_filter.shape), still(mine)],
        ),
        out_shape=[jax.ShapeDtypeStruct(short_filter.shape, F32), jax.ShapeDtypeStruct(mine, F32)],
        name="finish",
        compiler_params=room,
    )(place, total, other)
    return grad_query, grad_key, grad_value, grad_short, grad_medium


def solution(mesh):
    in_specs = (
        P("seq", "fsdp"),
        P("seq", "fsdp"),
        P("seq", "fsdp"),
        P("seq", "fsdp"),
        P(None, None, "fsdp"),
        P("fsdp", None),
    )
    out_specs = (
        P("seq", "fsdp"),
        P("seq", "fsdp"),
        P("seq", "fsdp"),
        P(None, None, "fsdp"),
        P("fsdp", None),
    )
    return jax.shard_map(shards, mesh=mesh, in_specs=in_specs, out_specs=out_specs, check_vma=False)
```

```python
import numpy as np
import jax
import jax.numpy as jnp
from jax import lax
from jax.experimental import pallas as pl
from jax.experimental.pallas import tpu as pltpu
from jax.sharding import PartitionSpec as P


HALO = 8
BLOCK = 128
WINDOW = 2 * BLOCK
F32 = jnp.float32
BF16 = jnp.bfloat16


def transforms():
    time = np.arange(WINDOW)
    freq = np.arange(BLOCK)
    angle = 2 * np.pi * ((freq[:, None] * time[None, :]) % WINDOW) / WINDOW
    cosine, sine = np.cos(angle), np.sin(angle)
    nyquist = np.where(time % 2 == 0, 1.0, -1.0)
    forward = np.concatenate([cosine, -sine]).astype(np.float64)
    forward[BLOCK] = nyquist
    scale = np.full(WINDOW, 2.0 / WINDOW)
    scale[0] = scale[BLOCK] = 1.0 / WINDOW
    inverse = forward.T * scale[None, :]
    forward = np.asarray(forward.astype(np.float32).astype(BF16))
    inverse = np.asarray(inverse.astype(np.float32).astype(BF16))
    return forward, forward[:, :BLOCK].copy(), inverse[:BLOCK], inverse[BLOCK:]


def dot(left, right):
    return jnp.dot(left, right, preferred_element_type=F32)


def to_spectrum(matrix, rows):
    return dot(matrix, rows)


def from_spectrum(matrix, real, imag):
    whole = jnp.concatenate([real, imag], axis=0).astype(BF16)
    return to_spectrum(matrix, whole)


def times(spec, taps):
    xr, xi = spec[:BLOCK], spec[BLOCK:]
    return xr * taps[0] - xi * taps[1], xr * taps[1] + xi * taps[2]


def times_conj(spec, taps):
    xr, xi = spec[:BLOCK], spec[BLOCK:]
    return xr * taps[0] + xi * taps[1], xi * taps[2] - xr * taps[1]


def blocks(wide, width):
    return [slice(at, at + width) for at in range(0, wide, width)]


def rounded(value):
    return value.astype(BF16).astype(F32)


LANES = 128
ROOM = 20 * 1024 * 1024
CHUNK = 64


def halves(width):
    return [(at // LANES, slice(at, at + LANES)) for at in range(0, width, LANES)]


def pieces(count):
    return [(at, min(CHUNK, count - at)) for at in range(0, count, CHUNK)]


def put(ref, at, value, lane=0):
    for h, lanes in halves(value.shape[1]):
        ref[h + lane // LANES, at : at + value.shape[0]] = value[:, lanes]


def causal(ref, h, at, count, weights):
    total = None
    for j, weight in enumerate(weights):
        term = weight * ref[h, at - j : at - j + count]
        total = term if total is None else total + term
    return total


def anticausal(ref, h, at, count, weights):
    total = None
    for j, weight in enumerate(weights):
        term = weight * ref[h, at + j : at + j + count]
        total = term if total is None else total + term
    return total


def taps_of(w, index, lanes):
    return [w[index, j : j + 1, lanes] for j in range(w.shape[1])]


def lag_sums(grad, g_at, x, x_at, h, count, taps):
    totals = [None] * taps
    for at, size in pieces(count):
        mine = grad[h, g_at + at : g_at + at + size]
        for j in range(taps):
            prod = mine * x[h, x_at + at - j : x_at + at - j + size]
            part = jnp.sum(prod.reshape(size // 8, 8, LANES), axis=0)
            totals[j] = part if totals[j] is None else totals[j] + part
    rows = [jnp.sum(t, axis=0, keepdims=True) for t in totals]
    return jnp.concatenate(rows + [jnp.zeros_like(rows[0])], axis=0)


def first_kernel(q, g, q_tail, k_tail, v_tail, k_head, v_head, w, tails, ahead, xq):
    tails[...] = jnp.concatenate(
        [x[...].astype(F32)[HALO:] for x in (q_tail, k_tail, v_tail)], axis=0
    ).astype(BF16)
    put(xq, 0, q[...].astype(F32))
    grad = g[...].astype(F32)
    heads = [x[: 2 * HALO, :].astype(F32)[:HALO] for x in (q, k_head, v_head, g)]
    ahead[: 4 * HALO] = jnp.concatenate(heads, axis=0).astype(BF16)
    for h, lanes in halves(q.shape[1]):
        weights = taps_of(w, 0, lanes)
        for at, size in pieces(BLOCK):
            qs = causal(xq, h, HALO + at, size, weights)
            ahead[4 * HALO + at : 4 * HALO + at + size, lanes] = (
                grad[HALO + at : HALO + at + size, lanes] * qs
            ).astype(BF16)


def second_kernel(
    q, k, v, g, tails, w,
    gated_out, ggi_out, ks_out, vs_out, behind_out,
    xq, xk, xv,
):
    rows, width = q.shape
    tail = tails[...].astype(F32)
    for at, (ref, x) in enumerate(((xq, q), (xk, k), (xv, v))):
        put(ref, 0, tail[at * HALO : (at + 1) * HALO])
        put(ref, HALO, x[...].astype(F32))
    for h, lanes in halves(width):
        wq, wk, wv = (taps_of(w, i, lanes) for i in range(3))
        for at, size in pieces(rows):
            span = slice(at, at + size)
            ks = causal(xk, h, HALO + at, size, wk)
            vs = causal(xv, h, HALO + at, size, wv)
            ks_out[span, lanes] = ks
            vs_out[span, lanes] = vs
            gated_out[span, lanes] = (ks * vs).astype(BF16)
            qs = causal(xq, h, HALO + at, size, wq)
            ggi_out[span, lanes] = (g[span, lanes].astype(F32) * qs).astype(BF16)
    behind_out[...] = gated_out[rows - BLOCK :, :]


def middle_kernel(me, _, q, g, gated, w, half, whole, high, own_taps, *refs):
    *more_taps, gq_out, next_out, sums_out, more_out, spec_out, rows_out, xq, yq, spec, taps = refs
    rows, width = gated.shape
    rest = rows - BLOCK
    groups = taps.shape[0]

    @pl.when(pl.program_id(0) == 0)
    def _():
        mine = own_taps.shape[0]
        share = groups // mine
        for at, part in enumerate([own_taps] + more_taps):
            start = lax.rem(me[0] + share - at, share) * mine
            taps[pl.ds(pl.multiple_of(start, mine), mine)] = part[...].astype(BF16).astype(F32)
        whole_taps = taps[...].astype(BF16)
        both = whole_taps
        whole_spec = lax.dot_general(
            half[...], both, (((1,), (1,)), ((), ())), preferred_element_type=F32
        )
        real, imag = whole_spec[:BLOCK], whole_spec[BLOCK:]
        first = lax.broadcasted_iota(jnp.int32, real.shape, 0) == 0
        spec[0] = real
        spec[1] = jnp.where(first, 0.0, imag)
        spec[2] = jnp.where(first, imag, real)
        spec_out[...] = spec[...]
        rows_out[...] = taps[...].T[:HALO]

    for lanes in blocks(width, groups):
        pad = jnp.zeros((WINDOW - rows, groups), BF16)
        window = jnp.concatenate([gated[:, lanes], pad], axis=0)
        prod = times(to_spectrum(whole[...], window), spec)
        sig = from_spectrum(high[: rest + HALO, :], *prod)
        put(yq, 0, rounded(g[:, lanes].astype(F32) * sig[:rest]), lanes.start)
        more_out[:, lanes] = sig[rest:]
    put(xq, 0, q[BLOCK - 2 * HALO :, :].astype(F32))
    for h, lanes in halves(width):
        next_out[:HALO, lanes] = yq[h, :HALO]
        next_out[HALO:, lanes] = yq[h, rest - HALO : rest]
        gq_out[:, lanes] = anticausal(yq, h, 0, rest, taps_of(w, 0, lanes)).astype(BF16)
        sums_out[:, lanes] = lag_sums(yq, 0, xq, 2 * HALO, h, rest, w.shape[1])


def third_kernel(
    me, k, v, tails, ends, ahead, gated, ggi, ks, vs, more, taps, w, spec, half, whole, low,
    gk_out, gv_out, next_out, sums_out, own_out, *rest_refs,
):
    *more_out, xe, xk, xv, yk, yv, acc, mscr = rest_refs
    rows, width = k.shape
    groups = spec.shape[2]
    rest = rows - BLOCK
    step = pl.program_id(0)
    count = w.shape[1]

    @pl.when(step == 0)
    def _():
        acc[...] = jnp.zeros_like(acc)

    head = ahead[: 4 * HALO, :].astype(F32)
    tail = tails[...].astype(F32)
    end = ends[...].astype(F32)
    for at in range(3):
        put(xe.at[at], HALO, end[at * HALO : (at + 1) * HALO])
        put(xe.at[at], 2 * HALO, head[at * HALO : (at + 1) * HALO])
        put(xe.at[at], 0, jnp.zeros((HALO, width), F32))
    news = [[], [], []]
    for h, lanes in halves(width):
        for at in range(3):
            news[at].append(causal(xe.at[at], h, 2 * HALO, HALO, taps_of(w, at, lanes)))
    qs_new, ks_new, vs_new = (jnp.concatenate(x, axis=1) for x in news)
    gated_new = rounded(ks_new * vs_new)
    ggi_new = head[3 * HALO :] * qs_new
    put(xe.at[0], HALO, gated_new)
    for h, lanes in halves(width):
        total = more[:, lanes]
        for j in range(HALO):
            at = lanes.start % groups
            total = total + taps[j : j + 1, at : at + LANES] * xe[0, h, HALO - j : 2 * HALO - j]
        next_out[:, lanes] = rounded(head[3 * HALO :, lanes] * total)
    put(xk, 0, tail[HALO : 2 * HALO])
    put(xk, HALO, k[...].astype(F32))
    put(xv, 0, tail[2 * HALO :])
    put(xv, HALO, v[...].astype(F32))
    fill = 3 * BLOCK - rows - HALO - BLOCK
    for lanes in blocks(width, groups):
        later = jnp.concatenate(
            [ggi_new[:, lanes], ahead[4 * HALO :, lanes].astype(F32), jnp.zeros((fill, groups), F32)],
            axis=0,
        ).astype(BF16)
        ggi_ext = jnp.concatenate([ggi[:, lanes], later], axis=0)
        own = jnp.concatenate([gated[:, lanes], jnp.zeros((WINDOW - rows, groups), BF16)], axis=0)
        for at in range(2):
            win = to_spectrum(whole[...], ggi_ext[at * BLOCK : at * BLOCK + WINDOW])
            gs = to_spectrum(half[...], own[at * BLOCK : (at + 1) * BLOCK])
            acc[0] += gs[:BLOCK] * win[:BLOCK]
            acc[1] += gs[BLOCK:] * win[BLOCK:]
            acc[2] += gs[:BLOCK] * win[BLOCK:] - gs[BLOCK:] * win[:BLOCK]
            prod = times_conj(win, spec)
            if at == 0:
                gg = from_spectrum(low[...], *prod)
                gk = (gg * vs[:BLOCK, lanes]).astype(BF16)
                gv = (gg * ks[:BLOCK, lanes]).astype(BF16)
                span = slice(0, BLOCK)
            else:
                gg = from_spectrum(low[: rest + HALO, :], *prod)
                zero = jnp.zeros((HALO, groups), F32)
                gk = jnp.concatenate(
                    [gg[:rest] * vs[BLOCK:, lanes], gg[rest:] * vs_new[:, lanes], zero], axis=0
                ).astype(BF16)
                gv = jnp.concatenate(
                    [gg[:rest] * ks[BLOCK:, lanes], gg[rest:] * ks_new[:, lanes], zero], axis=0
                ).astype(BF16)
                span = slice(BLOCK, rows + 2 * HALO)
            gk_out[span, lanes] = gk
            gv_out[span, lanes] = gv
            put(yk, span.start, gk.astype(F32), lanes.start)
            put(yv, span.start, gv.astype(F32), lanes.start)
        for h in range(lanes.start // LANES, lanes.stop // LANES):
            here = slice(h * LANES, (h + 1) * LANES)
            sums_out[:HALO, here] = lag_sums(yk, 0, xk, HALO, h, rows, count)
            sums_out[HALO:, here] = lag_sums(yv, 0, xv, HALO, h, rows, count)

    @pl.when(step == pl.num_programs(0) - 1)
    def _():
        first = lax.broadcasted_iota(jnp.int32, (BLOCK, groups), 0) == 0
        real = acc[0] + jnp.where(first, 0.0, acc[1])
        imag = jnp.where(first, acc[1], acc[2])
        mscr[...] = from_spectrum(low[...], real, imag).T
        mine = own_out.shape[0]
        share = groups // mine
        for at in range(share):
            part = mscr[pl.ds(pl.multiple_of(lax.rem(me[0] + at, share) * mine, mine), mine)]
            if at == 0:
                own_out[...] = part
            else:
                more_out[at - 1][...] = part.astype(BF16)


def fourth_kernel(gk, gv, near, far, w, gq_in, gk_out, gv_out, gq_out, yq, yk, yv):
    rows, width = gk_out.shape
    put(yk, 0, gk[...].astype(F32))
    put(yv, 0, gv[...].astype(F32))
    put(yq, 0, near[...])
    put(yq, HALO, far[...])
    put(yq, 2 * HALO, jnp.zeros((HALO, width), F32))
    old = gq_in[...].astype(F32)[:HALO]
    for h, lanes in halves(width):
        for i, ref, out in ((1, yk, gk_out), (2, yv, gv_out)):
            weights = taps_of(w, i, lanes)
            for at, size in pieces(rows):
                out[at : at + size, lanes] = anticausal(ref, h, at, size, weights).astype(BF16)
        fixed = anticausal(yq, h, 0, HALO, taps_of(w, 0, lanes))
        gq_out[:, lanes] = jnp.concatenate([old[:, lanes], fixed], axis=0).astype(BF16)


def pack_kernel(place, sums, own, *refs):
    *parts, keep_out, send_out, both = refs
    total = own[...]
    for part in parts:
        total = total + part[...].astype(F32)
    spread = halves(sums.shape[1])
    count = total.shape[0] // len(spread)
    both[: 2 * HALO] = sums[...]
    for h, lanes in spread:
        both[2 * HALO :, lanes] = total[h * count : (h + 1) * count]
    middle = sums.shape[1] // 2
    left, right = both[:, :middle], both[:, middle:]
    lower = lax.rem(place[0], 2) == 0
    keep_out[...] = jnp.where(lower, left, right)
    send_out[...] = jnp.where(lower, right, left).astype(BF16)


def fifth_kernel(
    q, tails, sums, g, gated, behind, spec, whole, high,
    yq_out, sums_out, send_out,
    xq, yq,
):
    width = q.shape[1]
    put(xq, 0, tails[...].astype(F32)[:HALO])
    put(xq, HALO, q[...].astype(F32))
    for lanes in blocks(width, spec.shape[2]):
        window = jnp.concatenate([behind[:, lanes], gated[:, lanes]], axis=0)
        sig = from_spectrum(high[...], *times(to_spectrum(whole[...], window), spec))
        grad = (g[:, lanes].astype(F32) * sig).astype(BF16)
        yq_out[:, lanes] = grad
        put(yq, 0, grad.astype(F32), lanes.start)
    for h, lanes in halves(width):
        sums_out[:, lanes] = sums[:, lanes] + lag_sums(yq, 0, xq, HALO, h, BLOCK, sums.shape[0] - 1)
    send_out[...] = sums_out[...].astype(BF16)


def sixth_kernel(grad, following, w, gq_in, gq_out, yq):
    put(yq, 0, grad[...].astype(F32))
    put(yq, BLOCK, following[...])
    for h, lanes in halves(grad.shape[1]):
        weights = taps_of(w, 0, lanes)
        for at, size in pieces(BLOCK):
            gq_out[at : at + size, lanes] = anticausal(yq, h, at, size, weights).astype(BF16)


def last_kernel(place, total, other, short_out, medium_out):
    lower = lax.rem(place[0], 2) == 0
    middle = total.shape[1]
    taps = short_out.shape[1]
    rows = total.shape[0] - 2 * HALO
    mine, theirs = total[...], other[...].astype(F32)
    late = mine[rows:] + theirs[rows:]
    sides = (
        jnp.where(lower, mine[:rows], theirs[:rows]),
        jnp.where(lower, theirs[:rows], mine[:rows]),
    )
    for at, part in enumerate(sides):
        here = slice(at * middle, (at + 1) * middle)
        short_out[0, :, here] = late[at * HALO : at * HALO + taps]
        short_out[1, :, here] = part[:taps]
        short_out[2, :, here] = part[HALO : HALO + taps]
        spread = halves(middle)
        count = rows - 2 * HALO
        for h, lanes in spread:
            place = (at * len(spread) + h) * count
            medium_out[place : place + count] = part[2 * HALO :, lanes]


def shift(value, axis, steps):
    count = lax.axis_size(axis)
    initial, last = (max(0, -steps), min(count, count - steps))
    return lax.ppermute(value, axis, [(s, s + steps) for s in range(initial, last)])


def exchanged(sends, axis):
    count = lax.axis_size(axis)
    return [
        lax.ppermute(part, axis, [(s, (s + step) % count) for s in range(count)])
        for step, part in enumerate(sends, 1)
    ]


def swap(value, axis, bit):
    count = lax.axis_size(axis)
    return lax.ppermute(value, axis, [(s, s ^ (1 << bit)) for s in range(count)])


def sums_over(kept, sent, late, sent_late, axis):
    count = lax.axis_size(axis)
    bits = count.bit_length() - 1
    middle = late.shape[1] // 2

    def stacked(value):
        return jnp.concatenate([value[:, :middle], value[:, middle:]], axis=0)

    early = kept + swap(sent, axis, 0).astype(F32)
    total = jnp.concatenate([early, stacked(late)], axis=0)
    sent = jnp.concatenate([early.astype(BF16), stacked(sent_late)], axis=0)
    for bit in range(bits - 1, 0, -1):
        total = total + swap(sent, axis, bit).astype(F32)
        sent = total.astype(BF16)
    return total, swap(sent, axis, 0)


def in_hbm(value):
    return pltpu.with_memory_space_constraint(value, pltpu.HBM)


def shards(query, key, value, grad_out, short_filter, medium_filter):
    rows, channels = query.shape
    groups = medium_filter.shape[0] * lax.axis_size("fsdp")
    width = groups
    rest = rows - BLOCK
    taps_short = short_filter.shape[1]
    whole, half, low, high = (jnp.asarray(m) for m in transforms())

    def col(count, at=0, wide=width):
        return pl.BlockSpec((count, wide), lambda i: (at, i))

    def filters(wide=width):
        return pl.BlockSpec((3, taps_short, wide), lambda i: (0, 0, i))

    def out(count, dtype):
        return jax.ShapeDtypeStruct((count, channels), dtype)

    def scratch(count, wide=width):
        return pltpu.VMEM((wide // LANES, count, LANES), F32)

    def cost(flops, moved):
        return pl.CostEstimate(flops=int(flops), bytes_accessed=int(moved), transcendentals=0)

    query, key, value, grad_out, short_filter = (
        in_hbm(x) for x in (query, key, value, grad_out, short_filter)
    )
    whole, half, low, high = (in_hbm(x) for x in (whole, half, low, high))
    room = pltpu.CompilerParams(vmem_limit_bytes=ROOM)
    wide = min(4 * width, channels)
    pair = min(2 * width, channels)
    last = rows // (2 * HALO) - 1
    ends, ahead = pl.pallas_call(
        first_kernel,
        grid=(channels // wide,),
        in_specs=[col(BLOCK + 2 * HALO, 0, wide)] * 2
        + [col(2 * HALO, last, wide)] * 3
        + [col(2 * HALO, 0, wide)] * 2
        + [filters(wide)],
        out_specs=[col(3 * HALO, 0, wide), col(BLOCK + 4 * HALO, 0, wide)],
        out_shape=[out(3 * HALO, BF16), out(BLOCK + 4 * HALO, BF16)],
        scratch_shapes=[scratch(BLOCK + 2 * HALO, wide)],
        name="first",
        compiler_params=room,
    )(query, grad_out, query, key, value, key, value, short_filter)
    tails = shift(ends, "seq", 1)
    ahead = shift(ahead, "seq", -1)
    share = lax.axis_size("fsdp")
    taps = exchanged([medium_filter.astype(BF16)] * (share - 1), "fsdp")

    gated, ggi, ks, vs, behind = pl.pallas_call(
        second_kernel,
        grid=(channels // wide,),
        in_specs=[col(rows, 0, wide)] * 4 + [col(3 * HALO, 0, wide), filters(wide)],
        out_specs=[col(rows, 0, wide)] * 4 + [col(BLOCK, 0, wide)],
        out_shape=[
            out(rows, BF16), out(rows, BF16), out(rows, F32), out(rows, F32), out(BLOCK, BF16),
        ],
        scratch_shapes=[scratch(rows + HALO, wide)] * 3,
        cost_estimate=cost(4e9, 20e6),
        name="second",
        compiler_params=room,
    )(query, key, value, grad_out, tails, short_filter)
    behind = shift(behind, "seq", 1)

    me = lax.axis_index("fsdp").astype(jnp.int32).reshape(1)
    place = lax.axis_index("seq").astype(jnp.int32).reshape(1)
    many = channels // wide

    def big(count, at=0):
        return pl.BlockSpec((count, wide), lambda i, *_: (at, i))

    def two(count, at=0):
        return pl.BlockSpec((count, pair), lambda i, *_: (at, i))

    def still(shape):
        return pl.BlockSpec(shape, lambda i, *_: (0,) * len(shape))

    two_filters = pl.BlockSpec((3, taps_short, pair), lambda i, *_: (0, 0, i))
    big_filters = pl.BlockSpec((3, taps_short, wide), lambda i, *_: (0, 0, i))
    corner = BLOCK // rest
    edge_block = rows // (2 * HALO) - 1
    grad_query, nexts, sums_q, more, spec, tap_rows = pl.pallas_call(
        middle_kernel,
        grid_spec=pltpu.PrefetchScalarGridSpec(
            num_scalar_prefetch=2,
            grid=(many,),
            in_specs=[big(rows), big(rest, corner), big(rows), big_filters]
            + [still(m.shape) for m in (half, whole, high)]
            + [still(medium_filter.shape)] * share,
            out_specs=[big(rest, corner), big(2 * HALO), big(HALO), big(HALO)]
            + [still((3, BLOCK, width)), still((HALO, width))],
            scratch_shapes=[scratch(rest + 2 * HALO, wide)] * 2
            + [pltpu.VMEM((3, BLOCK, width), F32), pltpu.VMEM((width, BLOCK), F32)],
        ),
        out_shape=[
            out(rows, BF16), out(2 * HALO, F32), out(HALO, F32), out(HALO, F32),
            jax.ShapeDtypeStruct((3, BLOCK, width), F32), jax.ShapeDtypeStruct((HALO, width), F32),
        ],
        cost_estimate=cost(4e9, 8e6),
        name="middle",
        compiler_params=room,
    )(me, place, query, grad_out, gated, short_filter, half, whole, high, medium_filter, *taps)

    mine = (width // share, BLOCK)
    gk, gv, far, sums_kv, own, *sends = pl.pallas_call(
        third_kernel,
        grid_spec=pltpu.PrefetchScalarGridSpec(
            num_scalar_prefetch=1,
            grid=(channels // pair,),
            in_specs=[two(rows)] * 2
            + [two(3 * HALO)] * 2
            + [two(BLOCK + 4 * HALO)]
            + [two(rows)] * 4
            + [two(HALO), still(tap_rows.shape), two_filters, still((3, BLOCK, width))]
            + [still(m.shape) for m in (half, whole, low)],
            out_specs=[two(rows + 2 * HALO)] * 2
            + [two(HALO)]
            + [two(2 * HALO)]
            + [still(mine)] * share,
            scratch_shapes=[pltpu.VMEM((3, pair // LANES, 3 * HALO, LANES), F32)]
            + [scratch(rows + 2 * HALO, pair)] * 4
            + [pltpu.VMEM((3, BLOCK, width), F32), pltpu.VMEM((width, BLOCK), F32)],
        ),
        out_shape=[out(rows + 2 * HALO, BF16)] * 2
        + [out(HALO, F32), out(2 * HALO, F32)]
        + [jax.ShapeDtypeStruct(mine, F32)]
        + [jax.ShapeDtypeStruct(mine, BF16)] * (share - 1),
        cost_estimate=cost(8e9, 20e6),
        name="third",
        compiler_params=room,
    )(me, key, value, tails, ends, ahead, gated, ggi, ks, vs, more, tap_rows,
      short_filter, spec, half, whole, low)
    parts = exchanged(sends, "fsdp")

    grad_key, grad_value, grad_query = pl.pallas_call(
        fourth_kernel,
        grid=(many,),
        in_specs=[big(rows + 2 * HALO)] * 2
        + [big(HALO, 1), big(HALO), big_filters, big(2 * HALO, edge_block)],
        out_specs=[big(rows), big(rows), big(2 * HALO, edge_block)],
        out_shape=[out(rows, BF16)] * 3,
        scratch_shapes=[scratch(3 * HALO, wide)] + [scratch(rows + 2 * HALO, wide)] * 2,
        input_output_aliases={5: 2},
        cost_estimate=cost(4e9, 10e6),
        name="fourth",
        compiler_params=room,
    )(gk, gv, nexts, far, short_filter, grad_query)

    extra = mine[0] * BLOCK // channels
    tall = (2 * HALO + extra, channels // 2)
    kept, sent = pl.pallas_call(
        pack_kernel,
        grid_spec=pltpu.PrefetchScalarGridSpec(
            num_scalar_prefetch=1,
            grid=(1,),
            in_specs=[still((2 * HALO, channels))] + [still(mine)] * share,
            out_specs=[still(tall)] * 2,
            scratch_shapes=[pltpu.VMEM((2 * HALO + extra, channels), F32)],
        ),
        out_shape=[jax.ShapeDtypeStruct(tall, F32), jax.ShapeDtypeStruct(tall, BF16)],
        name="pack",
        compiler_params=room,
    )(place, sums_kv, own, *parts)

    grads, sums_q, sent_q = pl.pallas_call(
        fifth_kernel,
        grid=(many,),
        in_specs=[big(BLOCK), big(3 * HALO), big(HALO)]
        + [big(BLOCK)] * 3
        + [still((3, BLOCK, width)), still(whole.shape), still(high.shape)],
        out_specs=[big(BLOCK), big(HALO), big(HALO)],
        out_shape=[out(BLOCK, BF16), out(HALO, F32), out(HALO, BF16)],
        scratch_shapes=[scratch(BLOCK + HALO, wide)] * 2,
        cost_estimate=cost(2e9, 8e6),
        name="fifth",
        compiler_params=room,
    )(query, tails, sums_q, grad_out, gated, behind, spec, whole, high)

    grad_query = pl.pallas_call(
        sixth_kernel,
        grid=(many,),
        in_specs=[big(BLOCK), big(HALO), big_filters, pl.BlockSpec(memory_space=pl.ANY)],
        out_specs=big(BLOCK),
        out_shape=out(rows, BF16),
        scratch_shapes=[scratch(BLOCK + HALO, wide)],
        input_output_aliases={3: 0},
        cost_estimate=cost(2e9, 3e6),
        name="sixth",
        compiler_params=room,
    )(grads, nexts, short_filter, grad_query)

    total, other = sums_over(kept, sent, sums_q, sent_q, "seq")
    grad_short, grad_medium = pl.pallas_call(
        last_kernel,
        grid_spec=pltpu.PrefetchScalarGridSpec(
            num_scalar_prefetch=1,
            grid=(1,),
            in_specs=[still(total.shape)] * 2,
            out_specs=[still(short_filter.shape), still(mine)],
        ),
        out_shape=[jax.ShapeDtypeStruct(short_filter.shape, F32), jax.ShapeDtypeStruct(mine, F32)],
        name="finish",
        compiler_params=room,
    )(place, total, other)
    return grad_query, grad_key, grad_value, grad_short, grad_medium


def solution(mesh):
    in_specs = (
        P("seq", "fsdp"),
        P("seq", "fsdp"),
        P("seq", "fsdp"),
        P("seq", "fsdp"),
        P(None, None, "fsdp"),
        P("fsdp", None),
    )
    out_specs = (
        P("seq", "fsdp"),
        P("seq", "fsdp"),
        P("seq", "fsdp"),
        P(None, None, "fsdp"),
        P("fsdp", None),
    )
    return jax.shard_map(shards, mesh=mesh, in_specs=in_specs, out_specs=out_specs, check_vma=False)
```
